32 devices in a mesh: dp: 4 (over z), table: 8 (over y, x, core).
Axes of the slice: x: 2, y: 2, z: 4, core: 2. Of those that a mesh axis runs over, the one named last changes fastest.
Arguments:
- item_emb: bfloat16 [16384, 512], P(('dp', 'table')), may hold values from -6 to 6
- cotangent: bfloat16 [16384, 512], P(('dp', 'table')), may hold values from -6 to 6
- in_proj: bfloat16 [512, 2048], replicated, may hold values from -0.25 to 0.25
- out_proj: bfloat16 [512, 512], replicated, may hold values from -0.25 to 0.25
- history_lengths: int32 [32, 8], P(('dp', 'table')), may hold values from 1 to 256, 512 in all within a row
- item_ids: int32 [16384], P(('dp', 'table')), may hold values from 0 to 32767, as said below
Outputs:
- emb_grad: float32 [32768, 512], P(('dp', 'table'))
- in_grad: float32 [512, 2048], replicated
- out_grad: float32 [512, 512], replicated
The draws below stay inside these ranges and needn't reach their ends.
Inputs may be any that keep to these rules, and one draw needn't show every extreme that they name: `item_ids`: among the 512 items of one device, at most 32 have ids of one device's rows (ids r with the same r // 1024), and these name at most 16 distinct ids; in every draw some device's rows get exactly 32 items with 16 distinct ids from every device. `history_lengths`: each row sums to 512.
All inputs are finite; a program needn't handle non-finite values.
Results may differ from the reference program's by a relative error of at most 0.0075.
Values sent between devices are 32-bit elements; how exact they have to be, the bound alone decides.
No kernel may reach another device: no remote copies, remote signals or barrier semaphores. Data moves between devices by JAX's collectives and lax.ppermute only.
A program may use at most 64 MiB of HBM per device.

```python
import math
import jax
import jax.numpy as jnp
import numpy as np
from jax import lax

D = 512
H = 4
TOK_DEV = 512
OWN_ROWS = 1024
SLOTS = 8
BLOCK = 512
LEN = 256
TOKENS = 16384
NBLK = 32
ROWS_ALL = 32768
CAP = 32
UCAP = 16
DEVICES = 32


def draw_item_ids(key, part):
    key_full, key_source = jax.random.split(key)
    total_slots = DEVICES * CAP
    full_owner = jax.random.randint(key_full, (), 0, DEVICES)

    def one_source(source_key):
        key_pick, key_offset, key_repeat, key_shuffle = jax.random.split(source_key, 4)
        priority = jax.random.permutation(key_pick, total_slots)
        slot_owner = jnp.arange(total_slots) // CAP
        priority = jnp.where(slot_owner == full_owner, -1, priority)
        chosen = jnp.argsort(priority, stable=True)[:TOK_DEV]
        owner_of = chosen // CAP
        within = chosen % CAP
        offsets = jax.random.randint(key_offset, (DEVICES,), 0, OWN_ROWS)
        repeats = jax.random.randint(key_repeat, (TOK_DEV,), 0, UCAP)
        distinct = jnp.where(within < UCAP, within, repeats)
        table_rows = owner_of * OWN_ROWS + (offsets[owner_of] + distinct) % OWN_ROWS
        return jax.random.permutation(key_shuffle, table_rows)
    source_keys = jax.random.split(key_source, DEVICES)
    return jax.vmap(one_source)(source_keys).reshape(-1).astype(jnp.int32)


def block_scale(rng, shape, shards, least, largest):
    def one(position, shards_of):
        heights = jax.random.uniform(jax.random.fold_in(jax.random.fold_in(rng, 6), position), (shards_of,), jnp.float32, least / len(shards), largest / len(shards))
        return jnp.repeat(jnp.exp(heights), shape[position] // shards_of).reshape((-1,) + (1,) * (len(shape) - position - 1))

    factor_of = one(*shards[0])
    for cut in shards[1:]:
        factor_of = factor_of * one(*cut)
    return factor_of


def split_up(number_of, total, reach, lean):
    portions = [(1 << 20) // math.isqrt(rank ** lean) + 1 for rank in range(2, number_of + 1)]
    spare, given = total - reach - (number_of - 1), [1] * (number_of - 1)
    while spare > 0:
        free = [i for i in range(number_of - 1) if given[i] < reach]
        whole, left = sum([portions[i] for i in free]), spare
        for i in free:
            more = min(reach - given[i], max(1, left * portions[i] // whole), spare)
            given[i] = given[i] + more
            spare = spare - more
    return np.array([reach] + given)


def ragged(stream_key, count, total, reach, skew):
    if count == 2:
        one = jax.random.randint(stream_key, (), max(1, total - reach), min(reach, total - 1) + 1)
        return jnp.stack([one, total - one])
    tallies = jnp.asarray(split_up(count, total, reach, skew), jnp.int32)
    pairs = (count - 1) // 2
    source_of, taker = tallies[1:1 + 2 * pairs:2], tallies[2:2 + 2 * pairs:2]
    slack = jnp.minimum(source_of - 1, reach - taker)
    passed = jax.random.randint(jax.random.fold_in(stream_key, 1), (pairs,), 0, 1 << 20) % (slack + 1)
    tallies = tallies.at[1:1 + 2 * pairs:2].set(source_of - passed).at[2:2 + 2 * pairs:2].set(taker + passed)
    return tallies[jax.random.permutation(jax.random.fold_in(stream_key, 2), count)]


def gaussian(own_key, extent, spread, bound, shards=(), kind=jnp.bfloat16):
    level = block_scale(own_key, extent, shards, -0.22, 0.18) if shards else 1.0
    values = jax.random.normal(own_key, extent, jnp.float32) * spread * level
    return jnp.minimum(jnp.maximum(values, -bound), bound).astype(kind)


def setup_inputs(seed: int = 0) -> dict:
    key_list = jax.random.split(jax.random.key(seed), 7)
    item_emb = gaussian(key_list[0], (TOKENS, D), 1.0, 6.0, ((0, 32),))
    cotangent = gaussian(key_list[1], (TOKENS, D), 1.0, 6.0, ((0, 32),))
    in_proj = gaussian(key_list[2], (D, 4 * D), D ** -0.5, 0.25)
    out_proj = gaussian(key_list[3], (D, D), D ** -0.5, 0.25)
    history_lengths = jax.vmap(lambda own: ragged(own, SLOTS, BLOCK, LEN, 2))(jax.random.split(key_list[4], NBLK)).reshape((NBLK, SLOTS)).astype(jnp.int32)
    item_ids = draw_item_ids(jax.random.fold_in(key_list[6], 71), 0)
    return {"item_emb": item_emb, "cotangent": cotangent, "in_proj": in_proj, "out_proj": out_proj, "history_lengths": history_lengths, "item_ids": item_ids}


norm_eps = 1e-05

def silu_grad(pre_value):
    sigmoid_z = jax.nn.sigmoid(pre_value)
    return sigmoid_z * (1.0 + pre_value * (1.0 - sigmoid_z))

def block_grads(item_rows, cot_rows, lengths, in_proj, out_proj):
    block_rows = item_rows.shape[0]
    model_width = item_rows.shape[1]
    head_size = model_width // H
    pre_act = jnp.dot(item_rows, in_proj, preferred_element_type=jnp.float32)
    hidden = jax.nn.silu(pre_act).astype(jnp.bfloat16)
    gating = hidden[:, :model_width].astype(jnp.float32)
    value_vecs = hidden[:, model_width:2 * model_width].reshape(block_rows, H, head_size).astype(jnp.float32)
    query_vecs = hidden[:, 2 * model_width:3 * model_width].reshape(block_rows, H, head_size).astype(jnp.float32)
    key_vecs = hidden[:, 3 * model_width:].reshape(block_rows, H, head_size).astype(jnp.float32)
    positions = jnp.arange(block_rows, dtype=jnp.int32)
    seq_ends = jnp.cumsum(lengths)
    segment = lax.optimization_barrier(jnp.sum((positions[:, None] >= seq_ends[None, :]).astype(jnp.int32), axis=1))
    causal_mask = ((segment[:, None] == segment[None, :]) & (positions[None, :] <= positions[:, None])).astype(jnp.float32) * (1.0 / LEN)
    score_scale = 1.0 / math.sqrt(head_size)
    scores = jnp.einsum('ihd,jhd->hij', query_vecs, key_vecs) * score_scale
    weights = (jax.nn.silu(scores) * causal_mask).astype(jnp.bfloat16)
    attended = jnp.einsum('hij,jhd->ihd', weights.astype(jnp.float32), value_vecs).reshape(block_rows, model_width)
    row_mean = lax.optimization_barrier(jnp.mean(attended, axis=1, keepdims=True))
    centered = attended - row_mean
    inv_std = lax.rsqrt(lax.optimization_barrier(jnp.mean(centered * centered, axis=1, keepdims=True)) + norm_eps)
    normed = centered * inv_std
    gated_out = (normed * gating).astype(jnp.bfloat16)
    grad_out = jnp.dot(cot_rows, out_proj.T, preferred_element_type=jnp.float32)
    grad_gate = grad_out * normed
    grad_norm = grad_out * gating
    grad_att = inv_std * (grad_norm - lax.optimization_barrier(jnp.mean(grad_norm, axis=1, keepdims=True)) - normed * lax.optimization_barrier(jnp.mean(grad_norm * normed, axis=1, keepdims=True)))
    grad_att = grad_att.astype(jnp.bfloat16).reshape(block_rows, H, head_size).astype(jnp.float32)
    grad_weights = jnp.einsum('ihd,jhd->hij', grad_att, value_vecs)
    grad_value = jnp.einsum('hij,ihd->jhd', weights.astype(jnp.float32), grad_att)
    grad_scores = (grad_weights * causal_mask * silu_grad(scores)).astype(jnp.bfloat16).astype(jnp.float32)
    grad_query = jnp.einsum('hij,jhd->ihd', grad_scores, key_vecs) * score_scale
    grad_key = jnp.einsum('hij,ihd->jhd', grad_scores, query_vecs) * score_scale
    grad_hidden = jnp.concatenate([grad_gate, grad_value.reshape(block_rows, model_width), grad_query.reshape(block_rows, model_width), grad_key.reshape(block_rows, model_width)], axis=1)
    grad_pre = (grad_hidden * silu_grad(pre_act)).astype(jnp.bfloat16)
    return (gated_out, grad_pre)

def reference(item_emb, cotangent, in_proj, out_proj, history_lengths, item_ids):

    def scan_step(totals, pieces):
        in_total, out_total = totals
        item_rows, cot_rows, lengths = pieces
        gated_out, grad_pre = block_grads(item_rows, cot_rows, lengths, in_proj, out_proj)
        out_total = out_total + jnp.dot(gated_out.T, cot_rows, preferred_element_type=jnp.float32)
        in_total = in_total + jnp.dot(item_rows.T, grad_pre, preferred_element_type=jnp.float32)
        item_grad = jnp.dot(grad_pre, in_proj.T, preferred_element_type=jnp.float32) + cot_rows.astype(jnp.float32)
        return ((in_total, out_total), item_grad)
    zero_sums = (jnp.zeros((D, 4 * D), jnp.float32), jnp.zeros((D, D), jnp.float32))
    pieces = (item_emb.reshape(NBLK, BLOCK, D), cotangent.reshape(NBLK, BLOCK, D), history_lengths)
    (in_total, out_total), item_grads = lax.scan(scan_step, zero_sums, pieces)
    grad_scale = 1.0 / math.sqrt(TOKENS)
    emb_grad = jnp.zeros((ROWS_ALL, D), jnp.float32).at[item_ids].add(item_grads.reshape(TOKENS, D))
    return (emb_grad, in_total * grad_scale, out_total * grad_scale)
```

```python
import functools
import math

import jax
import jax.numpy as jnp
from jax import lax
from jax.experimental import pallas as pl
from jax.experimental.pallas import tpu as pltpu
from jax.sharding import PartitionSpec as P

H = 4
OWN_ROWS = 1024
BLOCK = 512
LEN = 256
TILE = 256

norm_eps = 1e-05
VMEM = pltpu.MemorySpace.VMEM
SMEM = pltpu.MemorySpace.SMEM


def dot_nn(a, b):
    return lax.dot_general(a, b, (((1,), (0,)), ((), ())), preferred_element_type=jnp.float32)


def dot_nt(a, b):
    return lax.dot_general(a, b, (((1,), (1,)), ((), ())), preferred_element_type=jnp.float32)


def dot_tn(a, b):
    return lax.dot_general(a, b, (((0,), (0,)), ((), ())), preferred_element_type=jnp.float32)


def sigmoid(z):
    return 0.5 * jnp.tanh(0.5 * z) + 0.5


def block_kernel(lengths, emb, cot, in_proj, out_proj, gated_out, grad_pre, hid, dpre, mask, wts, dsc, att):
    rows, width = emb.shape
    head = width // H
    scale = 1.0 / math.sqrt(head)
    along_lane = lax.broadcasted_iota(jnp.int32, (1, rows), 1)
    along_row = lax.broadcasted_iota(jnp.int32, (rows, 1), 0)
    end = jnp.int32(0)
    seg_lane, seg_row = jnp.zeros_like(along_lane), jnp.zeros_like(along_row)
    for s in range(lengths.shape[1]):
        end = end + lengths[0, s]
        seg_lane = seg_lane + (along_lane >= end).astype(jnp.int32)
        seg_row = seg_row + (along_row >= end).astype(jnp.int32)
    for i in range(rows // TILE):
        r, n = pl.ds(i * TILE, TILE), (i + 1) * TILE
        own = seg_row[i * TILE : n] == seg_lane[:, :n]
        past = along_lane[:, :n] <= along_row[i * TILE : n]
        mask[r, :n] = jnp.where(own & past, 1.0 / LEN, 0.0)
    for c in range(4):
        cols = pl.ds(c * width, width)
        z = dot_nn(emb[...], in_proj[:, cols])
        sig = sigmoid(z)
        act = z * sig
        hid[:, cols] = act.astype(jnp.bfloat16)
        dpre[:, cols] = sig + act * (1.0 - sig)
    for h in range(H):
        v, q, k = (pl.ds((c * H + h) * head, head) for c in (1, 2, 3))
        for i in range(rows // TILE):
            r, n = pl.ds(i * TILE, TILE), (i + 1) * TILE
            m = mask[r, :n]
            s = dot_nt(hid[r, q], hid[:n, k]) * scale
            sig = sigmoid(s)
            act = s * sig
            w = (act * m).astype(jnp.bfloat16)
            wts[h, r, :n] = w
            dsc[h, r, :n] = (sig + act * (1.0 - sig)) * m
            att[r, pl.ds(h * head, head)] = dot_nn(w, hid[:n, v])
    grad_att = []
    for i in range(rows // TILE):
        r = pl.ds(i * TILE, TILE)
        a = att[r, :]
        centered = a - jnp.mean(a, axis=1, keepdims=True)
        inv_std = lax.rsqrt(jnp.mean(centered * centered, axis=1, keepdims=True) + norm_eps)
        normed = centered * inv_std
        gating = hid[r, :width].astype(jnp.float32)
        gated_out[r, :] = (normed * gating).astype(jnp.bfloat16)
        grad_out = dot_nt(cot[r, :], out_proj[...])
        grad_pre[r, :width] = (grad_out * normed * dpre[r, :width]).astype(jnp.bfloat16)
        grad_norm = grad_out * gating
        g = inv_std * (
            grad_norm
            - jnp.mean(grad_norm, axis=1, keepdims=True)
            - normed * jnp.mean(grad_norm * normed, axis=1, keepdims=True)
        )
        grad_att.append(g.astype(jnp.bfloat16))
    for h in range(H):
        v, q, k = (pl.ds((c * H + h) * head, head) for c in (1, 2, 3))
        grad_v, grad_k = [None] * (rows // TILE), [None] * (rows // TILE)
        for i in range(rows // TILE):
            r, n = pl.ds(i * TILE, TILE), (i + 1) * TILE
            g = grad_att[i][:, h * head : (h + 1) * head]
            gs = (dot_nt(g, hid[:n, v]) * dsc[h, r, :n]).astype(jnp.bfloat16)
            gq = dot_nn(gs, hid[:n, k]) * scale
            grad_pre[r, q] = (gq * dpre[r, q]).astype(jnp.bfloat16)
            for j in range(i + 1):
                cut = slice(j * TILE, (j + 1) * TILE)
                gv = dot_tn(wts[h, r, cut], g)
                gk = dot_tn(gs[:, cut], hid[r, q])
                grad_v[j] = gv if grad_v[j] is None else grad_v[j] + gv
                grad_k[j] = gk if grad_k[j] is None else grad_k[j] + gk
        for j in range(rows // TILE):
            r = pl.ds(j * TILE, TILE)
            grad_pre[r, v] = (grad_v[j] * dpre[r, v]).astype(jnp.bfloat16)
            grad_pre[r, k] = (grad_k[j] * scale * dpre[r, k]).astype(jnp.bfloat16)


def block_call(lengths, emb, cot, in_proj, out_proj):
    rows, width = emb.shape
    vmem = pl.BlockSpec(memory_space=VMEM)
    return pl.pallas_call(
        block_kernel,
        name="block",
        out_shape=(
            jax.ShapeDtypeStruct((rows, width), jnp.bfloat16),
            jax.ShapeDtypeStruct((rows, 4 * width), jnp.bfloat16),
        ),
        in_specs=[pl.BlockSpec(memory_space=SMEM)] + [vmem] * 4,
        out_specs=(vmem, vmem),
        scratch_shapes=[
            pltpu.VMEM((rows, 4 * width), jnp.bfloat16),
            pltpu.VMEM((rows, 4 * width), jnp.float32),
            pltpu.VMEM((rows, rows), jnp.float32),
            pltpu.VMEM((H, rows, rows), jnp.bfloat16),
            pltpu.VMEM((H, rows, rows), jnp.float32),
            pltpu.VMEM((rows, width), jnp.float32),
        ],
        compiler_params=pltpu.CompilerParams(vmem_limit_bytes=40 << 20),
    )(lengths, emb, cot, in_proj, out_proj)


def weight_kernel(chunk, place, emb, cot, gated_out, grad_pre, a_keep, b_keep, a_send, b_send, rel_a, rel_b, rel_g):
    width = emb.shape[1]
    half, rest = a_keep.shape
    emb_t, gated_t = emb[...].T, gated_out[...].T
    count = width // chunk
    for c in range(count):
        src = slice(c * chunk, (c + 1) * chunk)
        to_a = pl.ds(pl.multiple_of((c ^ place[0]) * chunk, chunk), chunk)
        to_b = pl.ds(pl.multiple_of((c ^ place[1]) * chunk, chunk), chunk)
        rel_a[to_a, :] = emb_t[src]
        rel_b[to_b, :] = emb_t[src]
        rel_g[to_b, :] = gated_t[src]
    in_b = 4 * width - rest
    for out_a, out_b, r in ((a_send, b_send, pl.ds(half, half)), (a_keep, b_keep, pl.ds(0, half))):
        out_a[...] = dot_nn(rel_a[r, :], grad_pre[:, :rest])
        out_b[:, :in_b] = dot_nn(rel_b[r, :], grad_pre[:, rest:])
        out_b[:, in_b:] = dot_nn(rel_g[r, :], cot[...])


def weight_call(chunk, place, emb, cot, gated_out, grad_pre):
    width = emb.shape[1]
    vmem = pl.BlockSpec(memory_space=VMEM)
    part = jax.ShapeDtypeStruct((width // 2, 5 * width // 2), jnp.float32)
    return pl.pallas_call(
        functools.partial(weight_kernel, chunk),
        name="weights",
        out_shape=(part,) * 4,
        in_specs=[pl.BlockSpec(memory_space=SMEM)] + [vmem] * 4,
        out_specs=(vmem,) * 4,
        scratch_shapes=[pltpu.VMEM((width, width), jnp.bfloat16)] * 3,
        compiler_params=pltpu.CompilerParams(vmem_limit_bytes=40 << 20),
    )(place, emb, cot, gated_out, grad_pre)


def split_bf16(x):
    high = x.astype(jnp.bfloat16)
    return high, (x - high.astype(jnp.float32)).astype(jnp.bfloat16)


def item_kernel(owners, slots, ids, cot, grad_pre, in_proj, sent):
    rows, width = cot.shape
    item_grad = dot_nt(grad_pre[...], in_proj[...]) + cot[...].astype(jnp.float32)
    high, low = split_bf16(item_grad)
    id_lane = ids[...]
    sub = lax.broadcasted_iota(jnp.int32, (rows, rows), 0)
    lane = lax.broadcasted_iota(jnp.int32, (rows, rows), 1)
    id_row = jnp.sum(jnp.where(sub == lane, id_lane, 0), axis=1, keepdims=True)
    repeat = jnp.max(jnp.where((id_row == id_lane) & (lane < sub), 1, 0), axis=1, keepdims=True)
    key = jnp.where(repeat == 0, id_row, jnp.int32(2**30))
    owner = id_lane // OWN_ROWS
    below = (key >= owner * OWN_ROWS) & (key < id_lane)
    rank = jnp.sum(jnp.where(below, 1, 0), axis=0, keepdims=True)
    slot = owner * slots + rank
    total = owners * slots
    pick = lax.broadcasted_iota(jnp.int32, (total, rows), 0) == slot
    onehot = jnp.where(pick, 1.0, 0.0).astype(jnp.bfloat16)
    summed = dot_nn(onehot, high) + dot_nn(onehot, low)
    for c in range(width // 128):
        sent[:, c * slots : (c + 1) * slots, :] = summed[:, c * 128 : (c + 1) * 128].reshape(owners, slots, 128)
    number = jnp.max(jnp.where(pick, id_lane - owner * OWN_ROWS, -1), axis=1, keepdims=True)
    number = jnp.broadcast_to(number.astype(jnp.float32), (total, 128)).reshape(owners, slots, 128)
    groups = slots // 8
    at = lax.broadcasted_iota(jnp.int32, (owners, 8, 128), 2) // (128 // groups)
    tail = number[:, :8]
    for g in range(1, groups):
        tail = jnp.where(at == g, number[:, g * 8 : (g + 1) * 8], tail)
    sent[:, (width // 128) * slots :, :] = tail


def item_call(owners, slots, ids, cot, grad_pre, in_proj):
    width = cot.shape[1]
    vmem = pl.BlockSpec(memory_space=VMEM)
    return pl.pallas_call(
        functools.partial(item_kernel, owners, slots),
        name="items",
        out_shape=jax.ShapeDtypeStruct((owners, (width // 128) * slots + 8, 128), jnp.float32),
        in_specs=[vmem] * 4,
        out_specs=vmem,
        compiler_params=pltpu.CompilerParams(vmem_limit_bytes=40 << 20),
    )(ids, cot, grad_pre, in_proj)


def table_kernel(owners, slots, got, emb_grad):
    width = emb_grad.shape[1]
    groups = slots // 8
    tail = got[:, (width // 128) * slots :, :]
    number = [tail[:, :, g * (128 // groups) : g * (128 // groups) + 1] for g in range(groups)]
    number = jnp.concatenate(number, axis=1).reshape(owners * slots, 1).astype(jnp.int32)
    pick = number == lax.broadcasted_iota(jnp.int32, (owners * slots, OWN_ROWS), 1)
    onehot = jnp.where(pick, 1.0, 0.0).astype(jnp.bfloat16).T
    for c in range(0, width // 128, 2):
        rows = [got[:, d * slots : (d + 1) * slots, :].reshape(owners * slots, 128) for d in (c, c + 1)]
        high, low = split_bf16(jnp.concatenate(rows, axis=1))
        emb_grad[:, c * 128 : (c + 2) * 128] = dot_nn(onehot, high) + dot_nn(onehot, low)


def table_call(owners, slots, got, width):
    vmem = pl.BlockSpec(memory_space=VMEM)
    return pl.pallas_call(
        functools.partial(table_kernel, owners, slots),
        name="table",
        out_shape=jax.ShapeDtypeStruct((OWN_ROWS, width), jnp.float32),
        in_specs=[vmem],
        out_specs=vmem,
        compiler_params=pltpu.CompilerParams(vmem_limit_bytes=40 << 20),
    )(got)


def place_kernel(count, chunk, place, *refs):
    pieces, (in_grad, out_grad), sems = refs[:-3], refs[-3:-1], refs[-1]
    width = in_grad.shape[0]
    rest = pieces[0].shape[1]
    in_b = 4 * width - rest
    copies = []
    for side in range(2):
        position = 0
        for piece in pieces[side * len(pieces) // 2 : (side + 1) * len(pieces) // 2]:
            for c in range(piece.shape[0] // chunk):
                row = pl.ds(pl.multiple_of((position ^ place[side]) * chunk, chunk), chunk)
                src = piece.at[pl.ds(c * chunk, chunk)]
                if side == 0:
                    copies.append((src, in_grad.at[row, pl.ds(0, rest)]))
                else:
                    copies.append((src.at[:, pl.ds(0, in_b)], in_grad.at[row, pl.ds(rest, in_b)]))
                    copies.append((src.at[:, pl.ds(in_b, width)], out_grad.at[row, :]))
                position += 1
    copies = [pltpu.make_async_copy(s, d, sems.at[i]) for i, (s, d) in enumerate(copies)]
    for c in copies:
        c.start()
    for c in copies:
        c.wait()


def place_call(chunk, place, pieces, width):
    count = width // chunk
    return pl.pallas_call(
        functools.partial(place_kernel, count, chunk),
        name="place",
        out_shape=(
            jax.ShapeDtypeStruct((width, 4 * width), jnp.float32),
            jax.ShapeDtypeStruct((width, width), jnp.float32),
        ),
        in_specs=[pl.BlockSpec(memory_space=SMEM)] + [pl.BlockSpec(memory_space=VMEM)] * len(pieces),
        out_specs=(pl.BlockSpec(memory_space=pl.ANY),) * 2,
        scratch_shapes=[pltpu.SemaphoreType.DMA((3 * count,))],
        compiler_params=pltpu.CompilerParams(vmem_limit_bytes=40 << 20),
    )(place, *pieces)


def swap(x, axis, distance):
    size = lax.axis_size(axis)
    return lax.ppermute(x, axis, [(i, i ^ distance) for i in range(size)])


def orders(table_count):
    bits = [1 << b for b in range(table_count.bit_length() - 1)]
    first, rest = bits[:1], bits[1:]
    cut = len(rest) // 2
    return first + rest, first + rest[cut:] + rest[:cut]


def position(order, index):
    at = jnp.int32(0)
    for bit in order:
        at = 2 * at + (index // bit) % 2
    return at


def halve(x):
    n = x.shape[0] // 2
    return x[:n], x[n:]


def per_device(item_emb, cotangent, in_proj, out_proj, history_lengths, item_ids):
    rows_here, width = item_emb.shape
    dp_count = lax.axis_size("dp")
    table_count = lax.axis_size("table")
    owners = dp_count * table_count
    slots = max(8, rows_here // owners)
    order_a, order_b = orders(table_count)
    table_index, dp_index = lax.axis_index("table"), lax.axis_index("dp")
    place = jnp.stack([position(order_a, table_index), position(order_b, table_index)])
    chunk = width // table_count

    gated_out, grad_pre = block_call(history_lengths, item_emb, cotangent, in_proj, out_proj)
    a_keep, b_keep, a_send, b_send = weight_call(chunk, place, item_emb, cotangent, gated_out, grad_pre)
    sent = item_call(owners, slots, item_ids.reshape(1, rows_here), cotangent, grad_pre, in_proj)

    for step, (bit_a, bit_b) in enumerate(zip(order_a, order_b)):
        a_got, b_got = swap(a_send, "table", bit_a), swap(b_send, "table", bit_b)
        a_sum, b_sum = a_keep + a_got, b_keep + b_got
        if step + 1 < len(order_a):
            (a_keep, a_send), (b_keep, b_send) = halve(a_sum), halve(b_sum)
    got = lax.all_to_all(sent, ("dp", "table"), split_axis=0, concat_axis=0, tiled=True)

    cut = 2 * a_sum.shape[1] // dp_count
    pieces = [x[:, i * cut : (i + 1) * cut] for x in (a_sum, b_sum) for i in range(dp_count // 2)]
    pieces = jnp.stack(pieces)
    mine = lambda d: lax.dynamic_index_in_dim(pieces, dp_index ^ d, 0, keepdims=False)
    total = mine(0)
    for d in range(1, dp_count):
        total = total + swap(mine(d), "dp", d)
    total = total * (1.0 / math.sqrt(rows_here * owners))
    whole = [total] + [swap(total, "dp", d) for d in range(1, dp_count)]
    whole = jnp.stack(whole)
    whole = [lax.dynamic_index_in_dim(whole, dp_index ^ d, 0, keepdims=False) for d in range(dp_count)]
    a = [jnp.concatenate(whole[: dp_count // 2], axis=1)]
    b = [jnp.concatenate(whole[dp_count // 2 :], axis=1)]

    for bit_a, bit_b in zip(order_a[::-1], order_b[::-1]):
        join = lambda x: x[0] if len(x) == 1 else jnp.concatenate(x, axis=0)
        a, b = [join(a)], [join(b)]
        a.append(swap(a[0], "table", bit_a))
        b.append(swap(b[0], "table", bit_b))
    in_grad, out_grad = place_call(chunk, place, a + b, width)
    emb_grad = table_call(owners, slots, got, width)
    return (emb_grad, in_grad, out_grad)


def solution(mesh):
    placed = (
        P(("dp", "table"), None),
        P(("dp", "table"), None),
        P(),
        P(),
        P(("dp", "table"), None),
        P(("dp", "table")),
    )
    return jax.shard_map(
        per_device,
        mesh=mesh,
        in_specs=placed,
        out_specs=(P(("dp", "table"), None), P(), P()),
        check_vma=False,
    )
```

```python
import functools
import math

import jax
import jax.numpy as jnp
from jax import lax
from jax.experimental import pallas as pl
from jax.experimental.pallas import tpu as pltpu
from jax.sharding import PartitionSpec as P

H = 4
OWN_ROWS = 1024
BLOCK = 512
LEN = 256
TILE = 256

norm_eps = 1e-05
VMEM = pltpu.MemorySpace.VMEM
SMEM = pltpu.MemorySpace.SMEM
HBM = pltpu.MemorySpace.HBM


def dot_nn(a, b):
    return lax.dot_general(a, b, (((1,), (0,)), ((), ())), preferred_element_type=jnp.float32)


def dot_nt(a, b):
    return lax.dot_general(a, b, (((1,), (1,)), ((), ())), preferred_element_type=jnp.float32)


def dot_tn(a, b):
    return lax.dot_general(a, b, (((0,), (0,)), ((), ())), preferred_element_type=jnp.float32)


def sigmoid(z):
    return 0.5 * jnp.tanh(0.5 * z) + 0.5


def block_kernel(
    chunk, place, lengths, emb_hbm, cot_hbm, in_hbm, out_hbm,
    keep, send, grad_pre, rel_a, rel_b, rel_g,
    emb, cot, in_proj, out_proj, hid, dpre, mask, wts, dsc, att, gated_out, sems,
):
    rows, width = emb.shape
    head = width // H
    scale = 1.0 / math.sqrt(head)
    copies = [pltpu.make_async_copy(emb_hbm, emb, sems.at[0])]
    for c in range(4):
        cols = pl.ds(c * width, width)
        copies.append(pltpu.make_async_copy(in_hbm.at[:, cols], in_proj.at[:, cols], sems.at[1 + c]))
    copies.append(pltpu.make_async_copy(cot_hbm, cot, sems.at[5]))
    copies.append(pltpu.make_async_copy(out_hbm, out_proj, sems.at[6]))
    for c in copies:
        c.start()
    along_lane = lax.broadcasted_iota(jnp.int32, (1, rows), 1)
    along_row = lax.broadcasted_iota(jnp.int32, (rows, 1), 0)
    end = jnp.int32(0)
    seg_lane, seg_row = jnp.zeros_like(along_lane), jnp.zeros_like(along_row)
    for s in range(lengths.shape[1]):
        end = end + lengths[0, s]
        seg_lane = seg_lane + (along_lane >= end).astype(jnp.int32)
        seg_row = seg_row + (along_row >= end).astype(jnp.int32)
    for i in range(rows // TILE):
        r, n = pl.ds(i * TILE, TILE), (i + 1) * TILE
        own = seg_row[i * TILE : n] == seg_lane[:, :n]
        past = along_lane[:, :n] <= along_row[i * TILE : n]
        mask[r, :n] = jnp.where(own & past, 1.0 / LEN, 0.0)
    copies[0].wait()
    for c in range(4):
        cols = pl.ds(c * width, width)
        copies[1 + c].wait()
        z = dot_nn(emb[...], in_proj[:, cols])
        sig = sigmoid(z)
        act = z * sig
        hid[:, cols] = act.astype(jnp.bfloat16)
        dpre[:, cols] = sig + act * (1.0 - sig)
    emb_t = emb[...].T
    count = width // chunk
    for c in range(count):
        src = slice(c * chunk, (c + 1) * chunk)
        to_a = pl.ds(pl.multiple_of((c ^ place[0]) * chunk, chunk), chunk)
        to_b = pl.ds(pl.multiple_of((c ^ place[1]) * chunk, chunk), chunk)
        rel_a[to_a, :] = emb_t[src]
        rel_b[to_b, :] = emb_t[src]
    for h in range(H):
        v, q, k = (pl.ds((c * H + h) * head, head) for c in (1, 2, 3))
        for i in range(rows // TILE):
            r, n = pl.ds(i * TILE, TILE), (i + 1) * TILE
            m = mask[r, :n]
            s = dot_nt(hid[r, q], hid[:n, k]) * scale
            sig = sigmoid(s)
            act = s * sig
            w = (act * m).astype(jnp.bfloat16)
            wts[h, r, :n] = w
            dsc[h, r, :n] = (sig + act * (1.0 - sig)) * m
            att[r, pl.ds(h * head, head)] = dot_nn(w, hid[:n, v])
    copies[5].wait()
    copies[6].wait()
    grad_att = []
    for i in range(rows // TILE):
        r = pl.ds(i * TILE, TILE)
        a = att[r, :]
        centered = a - jnp.mean(a, axis=1, keepdims=True)
        inv_std = lax.rsqrt(jnp.mean(centered * centered, axis=1, keepdims=True) + norm_eps)
        normed = centered * inv_std
        gating = hid[r, :width].astype(jnp.float32)
        gated_out[r, :] = (normed * gating).astype(jnp.bfloat16)
        grad_out = dot_nt(cot[r, :], out_proj[...])
        grad_pre[r, :width] = (grad_out * normed * dpre[r, :width]).astype(jnp.bfloat16)
        grad_norm = grad_out * gating
        g = inv_std * (
            grad_norm
            - jnp.mean(grad_norm, axis=1, keepdims=True)
            - normed * jnp.mean(grad_norm * normed, axis=1, keepdims=True)
        )
        grad_att.append(g.astype(jnp.bfloat16))
    gated_t = gated_out[...].T
    for c in range(count):
        to_b = pl.ds(pl.multiple_of((c ^ place[1]) * chunk, chunk), chunk)
        rel_g[to_b, :] = gated_t[c * chunk : (c + 1) * chunk]
    for h in range(H):
        v, q, k = (pl.ds((c * H + h) * head, head) for c in (1, 2, 3))
        grad_v, grad_k = [None] * (rows // TILE), [None] * (rows // TILE)
        for i in range(rows // TILE):
            r, n = pl.ds(i * TILE, TILE), (i + 1) * TILE
            g = grad_att[i][:, h * head : (h + 1) * head]
            gs = (dot_nt(g, hid[:n, v]) * dsc[h, r, :n]).astype(jnp.bfloat16)
            gq = dot_nn(gs, hid[:n, k]) * scale
            grad_pre[r, q] = (gq * dpre[r, q]).astype(jnp.bfloat16)
            for j in range(i + 1):
                cut = slice(j * TILE, (j + 1) * TILE)
                gv = dot_tn(wts[h, r, cut], g)
                gk = dot_tn(gs[:, cut], hid[r, q])
                grad_v[j] = gv if grad_v[j] is None else grad_v[j] + gv
                grad_k[j] = gk if grad_k[j] is None else grad_k[j] + gk
        for j in range(rows // TILE):
            r = pl.ds(j * TILE, TILE)
            grad_pre[r, v] = (grad_v[j] * dpre[r, v]).astype(jnp.bfloat16)
            grad_pre[r, k] = (grad_k[j] * scale * dpre[r, k]).astype(jnp.bfloat16)
    half, cut = width // 2, keep.shape[1]
    for out, r in ((send, pl.ds(half, half)), (keep, pl.ds(0, half))):
        out[:half, :] = dot_nn(rel_a[r, :], grad_pre[:, :cut])
        out[half:, :] = dot_nn(rel_b[r, :], grad_pre[:, cut : 2 * cut])


def block_call(chunk, place, lengths, emb, cot, in_proj, out_proj):
    rows, width = emb.shape
    vmem = pl.BlockSpec(memory_space=VMEM)
    part = jax.ShapeDtypeStruct((width, 5 * width // 4), jnp.float32)
    square = jax.ShapeDtypeStruct((width, rows), jnp.bfloat16)
    return pl.pallas_call(
        functools.partial(block_kernel, chunk),
        name="block",
        out_shape=(part, part, jax.ShapeDtypeStruct((rows, 4 * width), jnp.bfloat16), square, square, square),
        in_specs=[pl.BlockSpec(memory_space=SMEM)] * 2 + [pl.BlockSpec(memory_space=HBM)] * 4,
        out_specs=(vmem,) * 6,
        scratch_shapes=[
            pltpu.VMEM((rows, width), jnp.bfloat16),
            pltpu.VMEM((rows, width), jnp.bfloat16),
            pltpu.VMEM((width, 4 * width), jnp.bfloat16),
            pltpu.VMEM((width, width), jnp.bfloat16),
            pltpu.VMEM((rows, 4 * width), jnp.bfloat16),
            pltpu.VMEM((rows, 4 * width), jnp.float32),
            pltpu.VMEM((rows, rows), jnp.float32),
            pltpu.VMEM((H, rows, rows), jnp.bfloat16),
            pltpu.VMEM((H, rows, rows), jnp.float32),
            pltpu.VMEM((rows, width), jnp.float32),
            pltpu.VMEM((rows, width), jnp.bfloat16),
            pltpu.SemaphoreType.DMA((7,)),
        ],
        compiler_params=pltpu.CompilerParams(vmem_limit_bytes=40 << 20),
    )(place, lengths, emb, cot, in_proj, out_proj)


def second_kernel(rel_a, rel_b, rel_g, cot, grad_pre, keep, send):
    width = cot.shape[1]
    half, cut = width // 2, keep.shape[1]
    inner = 4 * width - 3 * cut
    for out, r in ((send, pl.ds(half, half)), (keep, pl.ds(0, half))):
        out[:half, :] = dot_nn(rel_a[r, :], grad_pre[:, 2 * cut : 3 * cut])
        out[half:, :inner] = dot_nn(rel_b[r, :], grad_pre[:, 3 * cut :])
        out[half:, inner:] = dot_nn(rel_g[r, :], cot[...])


def second_call(rel_a, rel_b, rel_g, cot, grad_pre):
    width = cot.shape[1]
    vmem = pl.BlockSpec(memory_space=VMEM)
    part = jax.ShapeDtypeStruct((width, 5 * width // 4), jnp.float32)
    return pl.pallas_call(
        second_kernel,
        name="second",
        out_shape=(part, part),
        in_specs=[vmem] * 5,
        out_specs=(vmem,) * 2,
        compiler_params=pltpu.CompilerParams(vmem_limit_bytes=16 << 20),
    )(rel_a, rel_b, rel_g, cot, grad_pre)


def split_bf16(x):
    high = x.astype(jnp.bfloat16)
    return high, (x - high.astype(jnp.float32)).astype(jnp.bfloat16)


def item_kernel(owners, slots, ids, cot, grad_pre, in_proj, sent):
    rows, width = cot.shape
    item_grad = dot_nt(grad_pre[...], in_proj[...]) + cot[...].astype(jnp.float32)
    high, low = split_bf16(item_grad)
    id_lane = ids[...]
    sub = lax.broadcasted_iota(jnp.int32, (rows, rows), 0)
    lane = lax.broadcasted_iota(jnp.int32, (rows, rows), 1)
    id_row = jnp.sum(jnp.where(sub == lane, id_lane, 0), axis=1, keepdims=True)
    repeat = jnp.max(jnp.where((id_row == id_lane) & (lane < sub), 1, 0), axis=1, keepdims=True)
    key = jnp.where(repeat == 0, id_row, jnp.int32(2**30))
    owner = id_lane // OWN_ROWS
    below = (key >= owner * OWN_ROWS) & (key < id_lane)
    rank = jnp.sum(jnp.where(below, 1, 0), axis=0, keepdims=True)
    slot = owner * slots + rank
    total = owners * slots
    pick = lax.broadcasted_iota(jnp.int32, (total, rows), 0) == slot
    onehot = jnp.where(pick, 1.0, 0.0).astype(jnp.bfloat16)
    summed = dot_nn(onehot, high) + dot_nn(onehot, low)
    for c in range(width // 128):
        sent[:, c * slots : (c + 1) * slots, :] = summed[:, c * 128 : (c + 1) * 128].reshape(owners, slots, 128)
    number = jnp.max(jnp.where(pick, id_lane - owner * OWN_ROWS, -1), axis=1, keepdims=True)
    number = jnp.broadcast_to(number.astype(jnp.float32), (total, 128)).reshape(owners, slots, 128)
    groups = slots // 8
    at = lax.broadcasted_iota(jnp.int32, (owners, 8, 128), 2) // (128 // groups)
    tail = number[:, :8]
    for g in range(1, groups):
        tail = jnp.where(at == g, number[:, g * 8 : (g + 1) * 8], tail)
    sent[:, (width // 128) * slots :, :] = tail


def item_call(owners, slots, ids, cot, grad_pre, in_proj):
    width = cot.shape[1]
    vmem = pl.BlockSpec(memory_space=VMEM)
    return pl.pallas_call(
        functools.partial(item_kernel, owners, slots),
        name="items",
        out_shape=jax.ShapeDtypeStruct((owners, (width // 128) * slots + 8, 128), jnp.float32),
        in_specs=[vmem] * 4,
        out_specs=vmem,
        compiler_params=pltpu.CompilerParams(vmem_limit_bytes=40 << 20),
    )(ids, cot, grad_pre, in_proj)


def table_kernel(owners, slots, got, emb_grad):
    width = emb_grad.shape[1]
    groups = slots // 8
    tail = got[:, (width // 128) * slots :, :]
    number = [tail[:, :, g * (128 // groups) : g * (128 // groups) + 1] for g in range(groups)]
    number = jnp.concatenate(number, axis=1).reshape(owners * slots, 1).astype(jnp.int32)
    pick = number == lax.broadcasted_iota(jnp.int32, (owners * slots, OWN_ROWS), 1)
    onehot = jnp.where(pick, 1.0, 0.0).astype(jnp.bfloat16).T
    for c in range(0, width // 128, 2):
        rows = [got[:, d * slots : (d + 1) * slots, :].reshape(owners * slots, 128) for d in (c, c + 1)]
        high, low = split_bf16(jnp.concatenate(rows, axis=1))
        emb_grad[:, c * 128 : (c + 2) * 128] = dot_nn(onehot, high) + dot_nn(onehot, low)


def table_call(owners, slots, got, width):
    vmem = pl.BlockSpec(memory_space=VMEM)
    return pl.pallas_call(
        functools.partial(table_kernel, owners, slots),
        name="table",
        out_shape=jax.ShapeDtypeStruct((OWN_ROWS, width), jnp.float32),
        in_specs=[vmem],
        out_specs=vmem,
        compiler_params=pltpu.CompilerParams(vmem_limit_bytes=40 << 20),
    )(got)


def place_kernel(chunk, column, place, *refs):
    pieces, outs, sems = refs[:8], refs[-3:-1], refs[-1]
    in_grad, out_grad = outs
    cut = pieces[0].shape[1]
    copies = []
    for side in range(2):
        first = column + side * cut
        inner = min(cut, in_grad.shape[1] - first)
        position = 0
        for piece in pieces[side * 4 : side * 4 + 4]:
            for c in range(piece.shape[0] // chunk):
                row = pl.ds(pl.multiple_of((position ^ place[side]) * chunk, chunk), chunk)
                src = piece.at[pl.ds(c * chunk, chunk)]
                copies.append((src.at[:, pl.ds(0, inner)], in_grad.at[row, pl.ds(first, inner)]))
                if inner < cut:
                    copies.append((src.at[:, pl.ds(inner, cut - inner)], out_grad.at[row, :]))
                position += 1
    copies = [pltpu.make_async_copy(s, d, sems.at[i]) for i, (s, d) in enumerate(copies)]
    for c in copies:
        c.start()
    for c in copies:
        c.wait()


def place_call(chunk, column, place, pieces, width, grads):
    count = width // chunk
    anywhere = pl.BlockSpec(memory_space=HBM)
    return pl.pallas_call(
        functools.partial(place_kernel, chunk, column),
        name="place",
        out_shape=(
            jax.ShapeDtypeStruct((width, 4 * width), jnp.float32),
            jax.ShapeDtypeStruct((width, width), jnp.float32),
        ),
        in_specs=[pl.BlockSpec(memory_space=SMEM)] + [pl.BlockSpec(memory_space=VMEM)] * 8 + [anywhere] * len(grads),
        out_specs=(anywhere,) * 2,
        scratch_shapes=[pltpu.SemaphoreType.DMA((3 * count,))],
        input_output_aliases={9 + i: i for i in range(len(grads))},
        compiler_params=pltpu.CompilerParams(vmem_limit_bytes=16 << 20),
    )(place, *pieces, *grads)


def swap(x, axis, distance):
    size = lax.axis_size(axis)
    return lax.ppermute(x, axis, [(i, i ^ distance) for i in range(size)])


def orders(table_count):
    bits = [1 << b for b in range(table_count.bit_length() - 1)]
    first, rest = bits[:1], bits[1:]
    cut = len(rest) // 2
    return first + rest, first + rest[cut:] + rest[:cut]


def position(order, index):
    at = jnp.int32(0)
    for bit in order:
        at = 2 * at + (index // bit) % 2
    return at


def halve(x):
    n = x.shape[0] // 2
    return x[:n], x[n:]


def reduce_all(keep, send, order_a, order_b, scale):
    dp_count = lax.axis_size("dp")
    odd = lax.axis_index("dp") % 2 == 1
    a, b = halve(keep + swap(send, "table", order_a[0]))
    for bit_a, bit_b in zip(order_a[1:], order_b[1:]):
        (a_keep, a_send), (b_keep, b_send) = halve(a), halve(b)
        a = a_keep + swap(a_send, "table", bit_a)
        b = b_keep + swap(b_send, "table", bit_b)
    x = jnp.where(odd, b, a) + swap(jnp.where(odd, a, b), "dp", 1)
    distance = 2
    while distance < dp_count:
        x = x + swap(x, "dp", distance)
        distance *= 2
    x = x * scale
    other = swap(x, "dp", 1)
    a, b = jnp.where(odd, other, x), jnp.where(odd, x, other)
    for bit_a, bit_b in zip(order_a[:1:-1], order_b[:1:-1]):
        a = jnp.concatenate([a, swap(a, "table", bit_a)], axis=0)
        b = jnp.concatenate([b, swap(b, "table", bit_b)], axis=0)
    pieces = []
    for x, bit in ((a, order_a[1]), (b, order_b[1])):
        far = swap(x, "table", bit)
        pieces += [x, far, swap(x, "table", order_a[0]), swap(far, "table", order_a[0])]
    return pieces


def per_device(item_emb, cotangent, in_proj, out_proj, history_lengths, item_ids):
    rows_here, width = item_emb.shape
    table_count = lax.axis_size("table")
    owners = lax.axis_size("dp") * table_count
    slots = max(8, rows_here // owners)
    order_a, order_b = orders(table_count)
    table_index = lax.axis_index("table")
    place = jnp.stack([position(order_a, table_index), position(order_b, table_index)])
    chunk = width // table_count
    scale = 1.0 / math.sqrt(rows_here * owners)

    keep_e, send_e, grad_pre, *rel = block_call(
        chunk, place, history_lengths, item_emb, cotangent, in_proj, out_proj
    )
    keep_f, send_f = second_call(*rel, cotangent, grad_pre)
    sent = item_call(owners, slots, item_ids.reshape(1, rows_here), cotangent, grad_pre, in_proj)
    got = lax.all_to_all(sent, ("dp", "table"), split_axis=0, concat_axis=0, tiled=True)
    pieces_e = reduce_all(keep_e, send_e, order_a, order_b, scale)
    pieces_f = reduce_all(keep_f, send_f, order_a, order_b, scale)
    grads = place_call(chunk, 0, place, pieces_e, width, ())
    in_grad, out_grad = place_call(chunk, 2 * keep_e.shape[1], place, pieces_f, width, grads)
    emb_grad = table_call(owners, slots, got, width)
    return (emb_grad, in_grad, out_grad)


def solution(mesh):
    placed = (
        P(("dp", "table"), None),
        P(("dp", "table"), None),
        P(),
        P(),
        P(("dp", "table"), None),
        P(("dp", "table")),
    )
    return jax.shard_map(
        per_device,
        mesh=mesh,
        in_specs=placed,
        out_specs=(P(("dp", "table"), None), P(), P()),
        check_vma=False,
    )
```

```python
import functools
import math

import jax
import jax.numpy as jnp
from jax import lax
from jax.experimental import pallas as pl
from jax.experimental.pallas import tpu as pltpu
from jax.sharding import PartitionSpec as P

H = 4
OWN_ROWS = 1024
BLOCK = 512
LEN = 256
TILE = 256

norm_eps = 1e-05
VMEM = pltpu.MemorySpace.VMEM
SMEM = pltpu.MemorySpace.SMEM
HBM = pltpu.MemorySpace.HBM


def dot_nn(a, b):
    return lax.dot_general(a, b, (((1,), (0,)), ((), ())), preferred_element_type=jnp.float32)


def dot_nt(a, b):
    return lax.dot_general(a, b, (((1,), (1,)), ((), ())), preferred_element_type=jnp.float32)


def dot_tn(a, b):
    return lax.dot_general(a, b, (((0,), (0,)), ((), ())), preferred_element_type=jnp.float32)


def sigmoid(z):
    return 0.5 * jnp.tanh(0.5 * z) + 0.5


def block_kernel(
    chunk, place, lengths, emb_hbm, cot_hbm, in_hbm, out_hbm,
    keep, send, grad_pre, rel_a, rel_b, rel_g,
    emb, cot, in_proj, out_proj, hid, dpre, mask, wts, dsc, att, gated_out, sems,
):
    rows, width = emb.shape
    head = width // H
    scale = 1.0 / math.sqrt(head)
    copies = [pltpu.make_async_copy(emb_hbm, emb, sems.at[0])]
    for c in range(4):
        cols = pl.ds(c * width, width)
        copies.append(pltpu.make_async_copy(in_hbm.at[:, cols], in_proj.at[:, cols], sems.at[1 + c]))
    copies.append(pltpu.make_async_copy(cot_hbm, cot, sems.at[5]))
    copies.append(pltpu.make_async_copy(out_hbm, out_proj, sems.at[6]))
    for c in copies:
        c.start()
    along_lane = lax.broadcasted_iota(jnp.int32, (1, rows), 1)
    along_row = lax.broadcasted_iota(jnp.int32, (rows, 1), 0)
    end = jnp.int32(0)
    seg_lane, seg_row = jnp.zeros_like(along_lane), jnp.zeros_like(along_row)
    for s in range(lengths.shape[1]):
        end = end + lengths[0, s]
        seg_lane = seg_lane + (along_lane >= end).astype(jnp.int32)
        seg_row = seg_row + (along_row >= end).astype(jnp.int32)
    for i in range(rows // TILE):
        r, n = pl.ds(i * TILE, TILE), (i + 1) * TILE
        own = seg_row[i * TILE : n] == seg_lane[:, :n]
        past = along_lane[:, :n] <= along_row[i * TILE : n]
        mask[r, :n] = jnp.where(own & past, 1.0 / LEN, 0.0)
    copies[0].wait()
    for c in range(4):
        cols = pl.ds(c * width, width)
        copies[1 + c].wait()
        z = dot_nn(emb[...], in_proj[:, cols])
        sig = sigmoid(z)
        act = z * sig
        hid[:, cols] = act.astype(jnp.bfloat16)
        dpre[:, cols] = sig + act * (1.0 - sig)
    emb_t = emb[...].T
    count = width // chunk
    for c in range(count):
        src = slice(c * chunk, (c + 1) * chunk)
        to_a = pl.ds(pl.multiple_of((c ^ place[0]) * chunk, chunk), chunk)
        to_b = pl.ds(pl.multiple_of((c ^ place[1]) * chunk, chunk), chunk)
        rel_a[to_a, :] = emb_t[src]
        rel_b[to_b, :] = emb_t[src]
    for h in range(H):
        v, q, k = (pl.ds((c * H + h) * head, head) for c in (1, 2, 3))
        for i in range(rows // TILE):
            r, n = pl.ds(i * TILE, TILE), (i + 1) * TILE
            m = mask[r, :n]
            s = dot_nt(hid[r, q], hid[:n, k]) * scale
            sig = sigmoid(s)
            act = s * sig
            w = (act * m).astype(jnp.bfloat16)
            wts[h, r, :n] = w
            dsc[h, r, :n] = (sig + act * (1.0 - sig)) * m
            att[r, pl.ds(h * head, head)] = dot_nn(w, hid[:n, v])
    copies[5].wait()
    copies[6].wait()
    grad_att = []
    for i in range(rows // TILE):
        r = pl.ds(i * TILE, TILE)
        a = att[r, :]
        centered = a - jnp.mean(a, axis=1, keepdims=True)
        inv_std = lax.rsqrt(jnp.mean(centered * centered, axis=1, keepdims=True) + norm_eps)
        normed = centered * inv_std
        gating = hid[r, :width].astype(jnp.float32)
        gated_out[r, :] = (normed * gating).astype(jnp.bfloat16)
        grad_out = dot_nt(cot[r, :], out_proj[...])
        grad_pre[r, :width] = (grad_out * normed * dpre[r, :width]).astype(jnp.bfloat16)
        grad_norm = grad_out * gating
        g = inv_std * (
            grad_norm
            - jnp.mean(grad_norm, axis=1, keepdims=True)
            - normed * jnp.mean(grad_norm * normed, axis=1, keepdims=True)
        )
        grad_att.append(g.astype(jnp.bfloat16))
    gated_t = gated_out[...].T
    for c in range(count):
        to_b = pl.ds(pl.multiple_of((c ^ place[1]) * chunk, chunk), chunk)
        rel_g[to_b, :] = gated_t[c * chunk : (c + 1) * chunk]
    for h in range(H):
        v, q, k = (pl.ds((c * H + h) * head, head) for c in (1, 2, 3))
        grad_v, grad_k = [None] * (rows // TILE), [None] * (rows // TILE)
        for i in range(rows // TILE):
            r, n = pl.ds(i * TILE, TILE), (i + 1) * TILE
            g = grad_att[i][:, h * head : (h + 1) * head]
            gs = (dot_nt(g, hid[:n, v]) * dsc[h, r, :n]).astype(jnp.bfloat16)
            gq = dot_nn(gs, hid[:n, k]) * scale
            grad_pre[r, q] = (gq * dpre[r, q]).astype(jnp.bfloat16)
            for j in range(i + 1):
                cut = slice(j * TILE, (j + 1) * TILE)
                gv = dot_tn(wts[h, r, cut], g)
                gk = dot_tn(gs[:, cut], hid[r, q])
                grad_v[j] = gv if grad_v[j] is None else grad_v[j] + gv
                grad_k[j] = gk if grad_k[j] is None else grad_k[j] + gk
        for j in range(rows // TILE):
            r = pl.ds(j * TILE, TILE)
            grad_pre[r, v] = (grad_v[j] * dpre[r, v]).astype(jnp.bfloat16)
            grad_pre[r, k] = (grad_k[j] * scale * dpre[r, k]).astype(jnp.bfloat16)
    half, cut = width // 2, keep.shape[1]
    for out, r in ((send, pl.ds(half, half)), (keep, pl.ds(0, half))):
        out[:half, :] = dot_nn(rel_a[r, :], grad_pre[:, :cut])
        out[half:, :] = dot_nn(rel_b[r, :], grad_pre[:, cut : 2 * cut])


def block_call(chunk, place, lengths, emb, cot, in_proj, out_proj):
    rows, width = emb.shape
    vmem = pl.BlockSpec(memory_space=VMEM)
    part = jax.ShapeDtypeStruct((width, 5 * width // 4), jnp.float32)
    square = jax.ShapeDtypeStruct((width, rows), jnp.bfloat16)
    return pl.pallas_call(
        functools.partial(block_kernel, chunk),
        name="block",
        out_shape=(part, part, jax.ShapeDtypeStruct((rows, 4 * width), jnp.bfloat16), square, square, square),
        in_specs=[pl.BlockSpec(memory_space=SMEM)] * 2 + [pl.BlockSpec(memory_space=HBM)] * 4,
        out_specs=(vmem,) * 6,
        scratch_shapes=[
            pltpu.VMEM((rows, width), jnp.bfloat16),
            pltpu.VMEM((rows, width), jnp.bfloat16),
            pltpu.VMEM((width, 4 * width), jnp.bfloat16),
            pltpu.VMEM((width, width), jnp.bfloat16),
            pltpu.VMEM((rows, 4 * width), jnp.bfloat16),
            pltpu.VMEM((rows, 4 * width), jnp.float32),
            pltpu.VMEM((rows, rows), jnp.float32),
            pltpu.VMEM((H, rows, rows), jnp.bfloat16),
            pltpu.VMEM((H, rows, rows), jnp.float32),
            pltpu.VMEM((rows, width), jnp.float32),
            pltpu.VMEM((rows, width), jnp.bfloat16),
            pltpu.SemaphoreType.DMA((7,)),
        ],
        compiler_params=pltpu.CompilerParams(vmem_limit_bytes=40 << 20),
    )(place, lengths, *(pltpu.with_memory_space_constraint(x, HBM) for x in (emb, cot, in_proj, out_proj)))


def second_kernel(rel_a, rel_b, rel_g, cot, grad_pre, keep, send):
    width = cot.shape[1]
    half, cut = width // 2, keep.shape[1]
    inner = 4 * width - 3 * cut
    for out, r in ((send, pl.ds(half, half)), (keep, pl.ds(0, half))):
        out[:half, :] = dot_nn(rel_a[r, :], grad_pre[:, 2 * cut : 3 * cut])
        out[half:, :inner] = dot_nn(rel_b[r, :], grad_pre[:, 3 * cut :])
        out[half:, inner:] = dot_nn(rel_g[r, :], cot[...])


def second_call(rel_a, rel_b, rel_g, cot, grad_pre):
    width = cot.shape[1]
    vmem = pl.BlockSpec(memory_space=VMEM)
    part = jax.ShapeDtypeStruct((width, 5 * width // 4), jnp.float32)
    return pl.pallas_call(
        second_kernel,
        name="second",
        out_shape=(part, part),
        in_specs=[vmem] * 5,
        out_specs=(vmem,) * 2,
        compiler_params=pltpu.CompilerParams(vmem_limit_bytes=16 << 20),
    )(rel_a, rel_b, rel_g, cot, grad_pre)


def split_bf16(x):
    high = x.astype(jnp.bfloat16)
    return high, (x - high.astype(jnp.float32)).astype(jnp.bfloat16)


def item_kernel(owners, slots, ids, cot, grad_pre, in_proj, sent):
    rows, width = cot.shape
    item_grad = dot_nt(grad_pre[...], in_proj[...]) + cot[...].astype(jnp.float32)
    high, low = split_bf16(item_grad)
    id_lane = ids[...]
    sub = lax.broadcasted_iota(jnp.int32, (rows, rows), 0)
    lane = lax.broadcasted_iota(jnp.int32, (rows, rows), 1)
    id_row = jnp.sum(jnp.where(sub == lane, id_lane, 0), axis=1, keepdims=True)
    repeat = jnp.max(jnp.where((id_row == id_lane) & (lane < sub), 1, 0), axis=1, keepdims=True)
    key = jnp.where(repeat == 0, id_row, jnp.int32(2**30))
    owner = id_lane // OWN_ROWS
    below = (key >= owner * OWN_ROWS) & (key < id_lane)
    rank = jnp.sum(jnp.where(below, 1, 0), axis=0, keepdims=True)
    slot = owner * slots + rank
    total = owners * slots
    pick = lax.broadcasted_iota(jnp.int32, (total, rows), 0) == slot
    onehot = jnp.where(pick, 1.0, 0.0).astype(jnp.bfloat16)
    summed = dot_nn(onehot, high) + dot_nn(onehot, low)
    for c in range(width // 128):
        sent[:, c * slots : (c + 1) * slots, :] = summed[:, c * 128 : (c + 1) * 128].reshape(owners, slots, 128)
    number = jnp.max(jnp.where(pick, id_lane - owner * OWN_ROWS, -1), axis=1, keepdims=True)
    number = jnp.broadcast_to(number.astype(jnp.float32), (total, 128)).reshape(owners, slots, 128)
    groups = slots // 8
    at = lax.broadcasted_iota(jnp.int32, (owners, 8, 128), 2) // (128 // groups)
    tail = number[:, :8]
    for g in range(1, groups):
        tail = jnp.where(at == g, number[:, g * 8 : (g + 1) * 8], tail)
    sent[:, (width // 128) * slots :, :] = tail


def item_call(owners, slots, ids, cot, grad_pre, in_proj):
    width = cot.shape[1]
    vmem = pl.BlockSpec(memory_space=VMEM)
    return pl.pallas_call(
        functools.partial(item_kernel, owners, slots),
        name="items",
        out_shape=jax.ShapeDtypeStruct((owners, (width // 128) * slots + 8, 128), jnp.float32),
        in_specs=[vmem] * 4,
        out_specs=vmem,
        compiler_params=pltpu.CompilerParams(vmem_limit_bytes=16 << 20),
    )(ids, cot, grad_pre, in_proj)


def table_kernel(owners, slots, got, emb_grad):
    width = emb_grad.shape[1]
    groups = slots // 8
    tail = got[:, (width // 128) * slots :, :]
    number = [tail[:, :, g * (128 // groups) : g * (128 // groups) + 1] for g in range(groups)]
    number = jnp.concatenate(number, axis=1).reshape(owners * slots, 1).astype(jnp.int32)
    pick = number == lax.broadcasted_iota(jnp.int32, (owners * slots, OWN_ROWS), 1)
    onehot = jnp.where(pick, 1.0, 0.0).astype(jnp.bfloat16).T
    for c in range(0, width // 128, 2):
        rows = [got[:, d * slots : (d + 1) * slots, :].reshape(owners * slots, 128) for d in (c, c + 1)]
        high, low = split_bf16(jnp.concatenate(rows, axis=1))
        emb_grad[:, c * 128 : (c + 2) * 128] = dot_nn(onehot, high) + dot_nn(onehot, low)


def table_call(owners, slots, got, width):
    vmem = pl.BlockSpec(memory_space=VMEM)
    return pl.pallas_call(
        functools.partial(table_kernel, owners, slots),
        name="table",
        out_shape=jax.ShapeDtypeStruct((OWN_ROWS, width), jnp.float32),
        in_specs=[vmem],
        out_specs=vmem,
        compiler_params=pltpu.CompilerParams(vmem_limit_bytes=16 << 20),
    )(got)


def place_kernel(chunk, column, place, *refs):
    pieces, outs, sems = refs[:8], refs[-3:-1], refs[-1]
    in_grad, out_grad = outs
    cut = pieces[0].shape[1]
    copies = []
    for side in range(2):
        first = column + side * cut
        inner = min(cut, in_grad.shape[1] - first)
        position = 0
        for piece in pieces[side * 4 : side * 4 + 4]:
            for c in range(piece.shape[0] // chunk):
                row = pl.ds(pl.multiple_of((position ^ place[side]) * chunk, chunk), chunk)
                src = piece.at[pl.ds(c * chunk, chunk)]
                copies.append((src.at[:, pl.ds(0, inner)], in_grad.at[row, pl.ds(first, inner)]))
                if inner < cut:
                    copies.append((src.at[:, pl.ds(inner, cut - inner)], out_grad.at[row, :]))
                position += 1
    copies = [pltpu.make_async_copy(s, d, sems.at[i]) for i, (s, d) in enumerate(copies)]
    for c in copies:
        c.start()
    for c in copies:
        c.wait()


def place_call(chunk, column, place, pieces, width, grads):
    count = width // chunk
    anywhere = pl.BlockSpec(memory_space=HBM)
    return pl.pallas_call(
        functools.partial(place_kernel, chunk, column),
        name="place",
        out_shape=(
            jax.ShapeDtypeStruct((width, 4 * width), jnp.float32),
            jax.ShapeDtypeStruct((width, width), jnp.float32),
        ),
        in_specs=[pl.BlockSpec(memory_space=SMEM)] + [pl.BlockSpec(memory_space=VMEM)] * 8 + [anywhere] * len(grads),
        out_specs=(anywhere,) * 2,
        scratch_shapes=[pltpu.SemaphoreType.DMA((3 * count,))],
        input_output_aliases={9 + i: i for i in range(len(grads))},
        compiler_params=pltpu.CompilerParams(vmem_limit_bytes=16 << 20),
    )(place, *pieces, *grads)


def swap(x, axis, distance):
    size = lax.axis_size(axis)
    return lax.ppermute(x, axis, [(i, i ^ distance) for i in range(size)])


def orders(table_count):
    bits = [1 << b for b in range(table_count.bit_length() - 1)]
    first, rest = bits[:1], bits[1:]
    cut = len(rest) // 2
    return first + rest, first + rest[cut:] + rest[:cut]


def position(order, index):
    at = jnp.int32(0)
    for bit in order:
        at = 2 * at + (index // bit) % 2
    return at


def halve(x):
    n = x.shape[0] // 2
    return x[:n], x[n:]


def after(x, *others):
    return lax.optimization_barrier((x, *others))[0]


def apart(*xs):
    return lax.optimization_barrier(xs)


def reduce_all(keep, send, order_a, order_b, scale, first=()):
    dp_count = lax.axis_size("dp")
    odd = lax.axis_index("dp") % 2 == 1
    total = keep + swap(send, "table", order_a[0])
    n = total.shape[0] // 4
    a_keep, a_send, b_keep, b_send = apart(*(total[i * n : (i + 1) * n] for i in range(4)))
    arrived = ()
    for step, (bit_a, bit_b) in enumerate(zip(order_a[1:], order_b[1:])):
        if step:
            (a_keep, a_send), (b_keep, b_send) = halve(a), halve(b)
            a_keep, a_send = apart(a_keep, a_send)
            b_keep, b_send = apart(b_keep, b_send)
        elif first:
            a_send, b_send = after(a_send, first[0]), after(b_send, first[1])
        a_got, b_got = swap(a_send, "table", bit_a), swap(b_send, "table", bit_b)
        arrived = arrived or (a_got, b_got)
        a, b = a_keep + a_got, b_keep + b_got
    x = jnp.where(odd, b, a) + swap(jnp.where(odd, a, b), "dp", 1)
    distance = 2
    while distance < dp_count:
        x = x + swap(x, "dp", distance)
        distance *= 2
    x = x * scale
    other = swap(x, "dp", 1)
    a, b = jnp.where(odd, other, x), jnp.where(odd, x, other)
    for bit_a, bit_b in zip(order_a[:1:-1], order_b[:1:-1]):
        a, b = apart(a)[0], apart(b)[0]
        a = jnp.concatenate([a, swap(a, "table", bit_a)], axis=0)
        b = jnp.concatenate([b, swap(b, "table", bit_b)], axis=0)
    a, b = apart(a)[0], apart(b)[0]
    return arrived, (a, b), (swap(a, "table", order_a[1]), swap(b, "table", order_b[1]))


def both_cores(near, far, bit):
    pieces = []
    for a, b in zip(near, far):
        pieces += [a, b, swap(a, "table", bit), swap(b, "table", bit)]
    return pieces


def per_device(item_emb, cotangent, in_proj, out_proj, history_lengths, item_ids):
    rows_here, width = item_emb.shape
    table_count = lax.axis_size("table")
    owners = lax.axis_size("dp") * table_count
    slots = max(8, rows_here // owners)
    order_a, order_b = orders(table_count)
    table_index = lax.axis_index("table")
    place = jnp.stack([position(order_a, table_index), position(order_b, table_index)])
    chunk = width // table_count
    scale = 1.0 / math.sqrt(rows_here * owners)

    keep_e, send_e, grad_pre, *rel = block_call(
        chunk, place, history_lengths, item_emb, cotangent, in_proj, out_proj
    )
    keep_f, send_f = second_call(*rel, cotangent, grad_pre)
    sent = item_call(owners, slots, item_ids.reshape(1, rows_here), cotangent, grad_pre, in_proj)
    got = lax.all_to_all(sent, ("dp", "table"), split_axis=0, concat_axis=0, tiled=True)
    arrived, near_e, far_e = reduce_all(keep_e, send_e, order_a, order_b, scale)
    _, near_f, far_f = reduce_all(keep_f, send_f, order_a, order_b, scale, arrived)
    pieces_e = both_cores(near_e, far_e, order_a[0])
    grads = place_call(chunk, 0, place, pieces_e, width, ())
    emb_grad = table_call(owners, slots, got, width)
    far_f, grads, emb_grad = lax.optimization_barrier((far_f, grads, emb_grad))
    pieces_f = both_cores(near_f, far_f, order_a[0])
    in_grad, out_grad = place_call(chunk, 2 * keep_e.shape[1], place, pieces_f, width, grads)
    return (emb_grad, in_grad, out_grad)


def solution(mesh):
    placed = (
        P(("dp", "table"), None),
        P(("dp", "table"), None),
        P(),
        P(),
        P(("dp", "table"), None),
        P(("dp", "table")),
    )
    return jax.shard_map(
        per_device,
        mesh=mesh,
        in_specs=placed,
        out_specs=(P(("dp", "table"), None), P(), P()),
        check_vma=False,
    )
```

```python
import functools
import math

import jax
import jax.numpy as jnp
from jax import lax
from jax.experimental import pallas as pl
from jax.experimental.pallas import tpu as pltpu
from jax.sharding import PartitionSpec as P

H = 4
OWN_ROWS = 1024
BLOCK = 512
LEN = 256
TILE = 256

norm_eps = 1e-05
VMEM = pltpu.MemorySpace.VMEM
SMEM = pltpu.MemorySpace.SMEM
HBM = pltpu.MemorySpace.HBM


def dot_nn(a, b):
    return lax.dot_general(a, b, (((1,), (0,)), ((), ())), preferred_element_type=jnp.float32)


def dot_nt(a, b):
    return lax.dot_general(a, b, (((1,), (1,)), ((), ())), preferred_element_type=jnp.float32)


def dot_tn(a, b):
    return lax.dot_general(a, b, (((0,), (0,)), ((), ())), preferred_element_type=jnp.float32)


def sigmoid(z):
    return 0.5 * jnp.tanh(0.5 * z) + 0.5


def block_kernel(
    chunk, place, lengths, emb_hbm, cot_hbm, in_hbm, out_hbm,
    keep, send, grad_pre, rel_q, rel_r, rel_g,
    emb, cot, in_proj, out_proj, hid, dpre, mask, wts, dsc, att, gated_out, rel_p, sems,
):
    rows, width = emb.shape
    head = width // H
    scale = 1.0 / math.sqrt(head)
    copies = [pltpu.make_async_copy(emb_hbm, emb, sems.at[0])]
    for c in range(4):
        cols = pl.ds(c * width, width)
        copies.append(pltpu.make_async_copy(in_hbm.at[:, cols], in_proj.at[:, cols], sems.at[1 + c]))
    copies.append(pltpu.make_async_copy(cot_hbm, cot, sems.at[5]))
    copies.append(pltpu.make_async_copy(out_hbm, out_proj, sems.at[6]))
    for c in copies:
        c.start()
    along_lane = lax.broadcasted_iota(jnp.int32, (1, rows), 1)
    along_row = lax.broadcasted_iota(jnp.int32, (rows, 1), 0)
    end = jnp.int32(0)
    seg_lane, seg_row = jnp.zeros_like(along_lane), jnp.zeros_like(along_row)
    for s in range(lengths.shape[1]):
        end = end + lengths[0, s]
        seg_lane = seg_lane + (along_lane >= end).astype(jnp.int32)
        seg_row = seg_row + (along_row >= end).astype(jnp.int32)
    for i in range(rows // TILE):
        r, n = pl.ds(i * TILE, TILE), (i + 1) * TILE
        own = seg_row[i * TILE : n] == seg_lane[:, :n]
        past = along_lane[:, :n] <= along_row[i * TILE : n]
        mask[r, :n] = jnp.where(own & past, 1.0 / LEN, 0.0)
    copies[0].wait()
    for c in range(4):
        cols = pl.ds(c * width, width)
        copies[1 + c].wait()
        z = dot_nn(emb[...], in_proj[:, cols])
        sig = sigmoid(z)
        act = z * sig
        hid[:, cols] = act.astype(jnp.bfloat16)
        dpre[:, cols] = sig + act * (1.0 - sig)
    emb_t = emb[...].T
    count = width // chunk
    for c in range(count):
        for chain, rel in enumerate((rel_p, rel_q, rel_r)):
            rel[moved(c, place, chain, chunk), :] = emb_t[c * chunk : (c + 1) * chunk]
    for h in range(H):
        v, q, k = (pl.ds((c * H + h) * head, head) for c in (1, 2, 3))
        for i in range(rows // TILE):
            r, n = pl.ds(i * TILE, TILE), (i + 1) * TILE
            m = mask[r, :n]
            s = dot_nt(hid[r, q], hid[:n, k]) * scale
            sig = sigmoid(s)
            act = s * sig
            w = (act * m).astype(jnp.bfloat16)
            wts[h, r, :n] = w
            dsc[h, r, :n] = (sig + act * (1.0 - sig)) * m
            att[r, pl.ds(h * head, head)] = dot_nn(w, hid[:n, v])
    copies[5].wait()
    copies[6].wait()
    grad_att = []
    for i in range(rows // TILE):
        r = pl.ds(i * TILE, TILE)
        a = att[r, :]
        centered = a - jnp.mean(a, axis=1, keepdims=True)
        inv_std = lax.rsqrt(jnp.mean(centered * centered, axis=1, keepdims=True) + norm_eps)
        normed = centered * inv_std
        gating = hid[r, :width].astype(jnp.float32)
        gated_out[r, :] = (normed * gating).astype(jnp.bfloat16)
        grad_out = dot_nt(cot[r, :], out_proj[...])
        grad_pre[r, :width] = (grad_out * normed * dpre[r, :width]).astype(jnp.bfloat16)
        grad_norm = grad_out * gating
        g = inv_std * (
            grad_norm
            - jnp.mean(grad_norm, axis=1, keepdims=True)
            - normed * jnp.mean(grad_norm * normed, axis=1, keepdims=True)
        )
        grad_att.append(g.astype(jnp.bfloat16))
    gated_t = gated_out[...].T
    for c in range(count):
        rel_g[moved(c, place, 2, chunk), :] = gated_t[c * chunk : (c + 1) * chunk]
    for h in range(H):
        v, q, k = (pl.ds((c * H + h) * head, head) for c in (1, 2, 3))
        grad_v, grad_k = [None] * (rows // TILE), [None] * (rows // TILE)
        for i in range(rows // TILE):
            r, n = pl.ds(i * TILE, TILE), (i + 1) * TILE
            g = grad_att[i][:, h * head : (h + 1) * head]
            gs = (dot_nt(g, hid[:n, v]) * dsc[h, r, :n]).astype(jnp.bfloat16)
            gq = dot_nn(gs, hid[:n, k]) * scale
            grad_pre[r, q] = (gq * dpre[r, q]).astype(jnp.bfloat16)
            for j in range(i + 1):
                cut = slice(j * TILE, (j + 1) * TILE)
                gv = dot_tn(wts[h, r, cut], g)
                gk = dot_tn(gs[:, cut], hid[r, q])
                grad_v[j] = gv if grad_v[j] is None else grad_v[j] + gv
                grad_k[j] = gk if grad_k[j] is None else grad_k[j] + gk
        for j in range(rows // TILE):
            r = pl.ds(j * TILE, TILE)
            grad_pre[r, v] = (grad_v[j] * dpre[r, v]).astype(jnp.bfloat16)
            grad_pre[r, k] = (grad_k[j] * scale * dpre[r, k]).astype(jnp.bfloat16)
    half, cut = keep.shape
    keep[...] = dot_nn(rel_p[:half, :], grad_pre[:, :cut])
    send[...] = dot_nn(rel_p[half:, :], grad_pre[:, :cut])


def moved(c, place, chain, chunk):
    return pl.ds(pl.multiple_of((c ^ place[chain]) * chunk, chunk), chunk)


def block_call(chunk, cut, place, lengths, emb, cot, in_proj, out_proj):
    rows, width = emb.shape
    vmem = pl.BlockSpec(memory_space=VMEM)
    part = jax.ShapeDtypeStruct((width // 2, cut), jnp.float32)
    square = jax.ShapeDtypeStruct((width, rows), jnp.bfloat16)
    return pl.pallas_call(
        functools.partial(block_kernel, chunk),
        name="block",
        out_shape=(part, part, jax.ShapeDtypeStruct((rows, 4 * width), jnp.bfloat16), square, square, square),
        in_specs=[pl.BlockSpec(memory_space=SMEM)] * 2 + [pl.BlockSpec(memory_space=HBM)] * 4,
        out_specs=(vmem,) * 6,
        scratch_shapes=[
            pltpu.VMEM((rows, width), jnp.bfloat16),
            pltpu.VMEM((rows, width), jnp.bfloat16),
            pltpu.VMEM((width, 4 * width), jnp.bfloat16),
            pltpu.VMEM((width, width), jnp.bfloat16),
            pltpu.VMEM((rows, 4 * width), jnp.bfloat16),
            pltpu.VMEM((rows, 4 * width), jnp.float32),
            pltpu.VMEM((rows, rows), jnp.float32),
            pltpu.VMEM((H, rows, rows), jnp.bfloat16),
            pltpu.VMEM((H, rows, rows), jnp.float32),
            pltpu.VMEM((rows, width), jnp.float32),
            pltpu.VMEM((rows, width), jnp.bfloat16),
            pltpu.VMEM((width, rows), jnp.bfloat16),
            pltpu.SemaphoreType.DMA((7,)),
        ],
        compiler_params=pltpu.CompilerParams(vmem_limit_bytes=28 << 20),
    )(place, lengths, *(pltpu.with_memory_space_constraint(x, HBM) for x in (emb, cot, in_proj, out_proj)))


def rest_kernel(first, rel_q, rel_r, rel_g, cot, grad_pre, keep_q, send_q, keep_r, send_r):
    half, cut = keep_q.shape
    at = first + cut
    inner = grad_pre.shape[1] - at
    for keep, r in ((keep_q, pl.ds(0, half)), (send_q, pl.ds(half, half))):
        keep[...] = dot_nn(rel_q[r, :], grad_pre[:, first:at])
    for keep, r in ((keep_r, pl.ds(0, half)), (send_r, pl.ds(half, half))):
        if inner:
            keep[:, :inner] = dot_nn(rel_r[r, :], grad_pre[:, at:])
        keep[:, inner:] = dot_nn(rel_g[r, :], cot[...])


def rest_call(cuts, rel_q, rel_r, rel_g, cot, grad_pre):
    width = cot.shape[1]
    vmem = pl.BlockSpec(memory_space=VMEM)
    part_q, part_r = (jax.ShapeDtypeStruct((width // 2, n), jnp.float32) for n in cuts[1:])
    return pl.pallas_call(
        functools.partial(rest_kernel, cuts[0]),
        name="rest",
        out_shape=(part_q, part_q, part_r, part_r),
        in_specs=[vmem] * 5,
        out_specs=(vmem,) * 4,
        compiler_params=pltpu.CompilerParams(vmem_limit_bytes=8 << 20),
    )(rel_q, rel_r, rel_g, cot, grad_pre)


def split_bf16(x):
    high = x.astype(jnp.bfloat16)
    return high, (x - high.astype(jnp.float32)).astype(jnp.bfloat16)


def item_kernel(owners, slots, ids, cot, grad_pre, in_proj, sent):
    rows, width = cot.shape
    item_grad = dot_nt(grad_pre[...], in_proj[...]) + cot[...].astype(jnp.float32)
    high, low = split_bf16(item_grad)
    id_lane = ids[...]
    sub = lax.broadcasted_iota(jnp.int32, (rows, rows), 0)
    lane = lax.broadcasted_iota(jnp.int32, (rows, rows), 1)
    id_row = jnp.sum(jnp.where(sub == lane, id_lane, 0), axis=1, keepdims=True)
    repeat = jnp.max(jnp.where((id_row == id_lane) & (lane < sub), 1, 0), axis=1, keepdims=True)
    key = jnp.where(repeat == 0, id_row, jnp.int32(2**30))
    owner = id_lane // OWN_ROWS
    below = (key >= owner * OWN_ROWS) & (key < id_lane)
    rank = jnp.sum(jnp.where(below, 1, 0), axis=0, keepdims=True)
    slot = owner * slots + rank
    total = owners * slots
    pick = lax.broadcasted_iota(jnp.int32, (total, rows), 0) == slot
    onehot = jnp.where(pick, 1.0, 0.0).astype(jnp.bfloat16)
    summed = dot_nn(onehot, high) + dot_nn(onehot, low)
    for c in range(width // 128):
        sent[:, c * slots : (c + 1) * slots, :] = summed[:, c * 128 : (c + 1) * 128].reshape(owners, slots, 128)
    number = jnp.max(jnp.where(pick, id_lane - owner * OWN_ROWS, -1), axis=1, keepdims=True)
    number = jnp.broadcast_to(number.astype(jnp.float32), (total, 128)).reshape(owners, slots, 128)
    groups = slots // 8
    at = lax.broadcasted_iota(jnp.int32, (owners, 8, 128), 2) // (128 // groups)
    tail = number[:, :8]
    for g in range(1, groups):
        tail = jnp.where(at == g, number[:, g * 8 : (g + 1) * 8], tail)
    sent[:, (width // 128) * slots :, :] = tail


def item_call(owners, slots, ids, cot, grad_pre, in_proj):
    width = cot.shape[1]
    vmem = pl.BlockSpec(memory_space=VMEM)
    return pl.pallas_call(
        functools.partial(item_kernel, owners, slots),
        name="items",
        out_shape=jax.ShapeDtypeStruct((owners, (width // 128) * slots + 8, 128), jnp.float32),
        in_specs=[vmem] * 4,
        out_specs=vmem,
        compiler_params=pltpu.CompilerParams(vmem_limit_bytes=8 << 20),
    )(ids, cot, grad_pre, in_proj)


def table_kernel(owners, slots, got, emb_grad):
    width = emb_grad.shape[1]
    groups = slots // 8
    tail = got[:, (width // 128) * slots :, :]
    number = [tail[:, :, g * (128 // groups) : g * (128 // groups) + 1] for g in range(groups)]
    number = jnp.concatenate(number, axis=1).reshape(owners * slots, 1).astype(jnp.int32)
    pick = number == lax.broadcasted_iota(jnp.int32, (owners * slots, OWN_ROWS), 1)
    onehot = jnp.where(pick, 1.0, 0.0).astype(jnp.bfloat16).T
    for c in range(0, width // 128, 2):
        rows = [got[:, d * slots : (d + 1) * slots, :].reshape(owners * slots, 128) for d in (c, c + 1)]
        high, low = split_bf16(jnp.concatenate(rows, axis=1))
        emb_grad[:, c * 128 : (c + 2) * 128] = dot_nn(onehot, high) + dot_nn(onehot, low)


def table_call(owners, slots, got, width):
    vmem = pl.BlockSpec(memory_space=VMEM)
    return pl.pallas_call(
        functools.partial(table_kernel, owners, slots),
        name="table",
        out_shape=jax.ShapeDtypeStruct((OWN_ROWS, width), jnp.float32),
        in_specs=[vmem],
        out_specs=vmem,
        compiler_params=pltpu.CompilerParams(vmem_limit_bytes=8 << 20),
    )(got)


def place_kernel(chunk, spots, place, *refs):
    pieces, (in_grad, out_grad), sems = refs[: len(spots)], refs[-3:-1], refs[-1]
    copies = []
    for piece, (chain, first, position) in zip(pieces, spots):
        cut = piece.shape[1]
        inner = min(cut, in_grad.shape[1] - first)
        for c in range(piece.shape[0] // chunk):
            row = moved(position + c, place, chain, chunk)
            src = piece.at[pl.ds(c * chunk, chunk)]
            if inner:
                copies.append((src.at[:, pl.ds(0, inner)], in_grad.at[row, pl.ds(first, inner)]))
            if inner < cut:
                copies.append((src.at[:, pl.ds(inner, cut - inner)], out_grad.at[row, :]))
    copies = [pltpu.make_async_copy(s, d, sems.at[i]) for i, (s, d) in enumerate(copies)]
    for c in copies:
        c.start()
    for c in copies:
        c.wait()


def place_call(chunk, spots, place, pieces, width, grads):
    anywhere = pl.BlockSpec(memory_space=HBM)
    vmem = pl.BlockSpec(memory_space=VMEM)
    return pl.pallas_call(
        functools.partial(place_kernel, chunk, spots),
        name="place",
        out_shape=(
            jax.ShapeDtypeStruct((width, 4 * width), jnp.float32),
            jax.ShapeDtypeStruct((width, width), jnp.float32),
        ),
        in_specs=[pl.BlockSpec(memory_space=SMEM)] + [vmem] * len(pieces) + [anywhere] * len(grads),
        out_specs=(anywhere,) * 2,
        scratch_shapes=[pltpu.SemaphoreType.DMA((4 * width // chunk,))],
        input_output_aliases={1 + len(pieces) + i: i for i in range(len(grads))},
        compiler_params=pltpu.CompilerParams(vmem_limit_bytes=2 << 20),
    )(place, *pieces, *grads)


def swap(x, where):
    axis, distance = where
    size = lax.axis_size(axis)
    return lax.ppermute(x, axis, [(i, i ^ distance) for i in range(size)])


def bits_of(axis):
    return [(axis, 1 << b) for b in range(lax.axis_size(axis).bit_length() - 1)]


def orders():
    table = bits_of("table")
    core, rest, z = table[:1], table[1:], bits_of("dp")
    x, y = rest[: len(rest) // 2], rest[len(rest) // 2 :]
    z, last = z[:-1], z[-1:]
    return core + x + y + z + last, core + y + z + x + last, core + z + x + y + last


def position(order):
    at = jnp.int32(0)
    for axis, distance in order:
        at = 2 * at + (lax.axis_index(axis) // distance) % 2
    return at


def after(x, *others):
    return lax.optimization_barrier((x, *others))[0]


def apart(*xs):
    return lax.optimization_barrier(xs)


def halve(x):
    n = x.shape[0] // 2
    return apart(x[:n], x[n:])


def exchange(keep, send, order, scale):
    x = keep + (yield swap(send, order[0]))
    for where in order[1:-1]:
        keep, send = halve(x)
        x = keep + (yield swap(send, where))
    x = (x + (yield swap(x, order[-1]))) * scale
    for where in order[-2:1:-1]:
        (x,) = apart(x)
        x = jnp.concatenate([x, (yield swap(x, where))], axis=0)
    (x,) = apart(x)
    return x, swap(x, order[1]), swap(x, order[0])


class Run:
    def __init__(self, steps):
        self.steps, self.count, self.pieces, self.last = steps, 0, None, ()
        self.waiting = next(steps)

    def advance(self, *others):
        here = after(self.waiting, *others)
        self.count, self.last = self.count + 1, (here,)
        try:
            self.waiting = self.steps.send(here)
        except StopIteration as stop:
            self.pieces = stop.value


CUTS = 8, 7, 5
ITEMS_AT, SENT_AT, GOT_AT, TABLE_AT, STRICT = 1, 1, 3, 4, 1


def per_device(item_emb, cotangent, in_proj, out_proj, history_lengths, item_ids):
    rows_here, width = item_emb.shape
    owners = lax.axis_size("dp") * lax.axis_size("table")
    slots = max(8, rows_here // owners)
    order = orders()
    place = jnp.stack([position(o[:-1]) for o in order])
    chunk = width >> (len(order[0]) - 1)
    scale = 1.0 / math.sqrt(rows_here * owners)
    cuts = [c * 5 * width // 20 for c in CUTS]

    *p, grad_pre, rel_q, rel_r, rel_g = block_call(
        chunk, cuts[0], place, history_lengths, item_emb, cotangent, in_proj, out_proj
    )
    q_keep, q_send, *r = rest_call(cuts, rel_q, rel_r, rel_g, cotangent, grad_pre)
    runs = [Run(exchange(*x, o, scale)) for x, o in zip((p, (q_keep, q_send), r), order)]
    hold, got, emb_grad = (), None, None
    while runs[-1].pieces is None:
        step = runs[0].count
        if step == ITEMS_AT:
            sent = item_call(owners, slots, item_ids.reshape(1, rows_here), cotangent, grad_pre, in_proj)
            hold = (sent,)
        if step == SENT_AT:
            got = lax.all_to_all(after(sent, *(runs[0].last if SENT_AT > ITEMS_AT else ())), ("dp", "table"), split_axis=0, concat_axis=0, tiled=True)
        if step == TABLE_AT:
            emb_grad = table_call(owners, slots, after(got, *runs[0].last), width)
            hold = (emb_grad,)
        if step == GOT_AT:
            hold = (got,)
        for run in runs:
            run.advance(*hold)
            hold = run.last if step >= STRICT else hold
        hold = hold if step >= STRICT else ()
    if emb_grad is None:
        emb_grad = table_call(owners, slots, got, width)
    near, far, beside = zip(*(run.pieces for run in runs))
    firsts = [sum(cuts[:chain]) for chain in range(len(cuts))]
    quarter = width // chunk // 4
    spots = lambda at: [(chain, first, at * quarter) for chain, first in enumerate(firsts)]
    grads = place_call(chunk, spots(0) + spots(2), place, near + beside, width, ())
    far = [after(x, *grads, emb_grad) for x in far]
    across = [swap(x, o[0]) for x, o in zip(far, order)]
    in_grad, out_grad = place_call(chunk, spots(1) + spots(3), place, far + across, width, grads)
    return (emb_grad, in_grad, out_grad)


def solution(mesh):
    placed = (
        P(("dp", "table"), None),
        P(("dp", "table"), None),
        P(),
        P(),
        P(("dp", "table"), None),
        P(("dp", "table")),
    )
    return jax.shard_map(
        per_device,
        mesh=mesh,
        in_specs=placed,
        out_specs=(P(("dp", "table"), None), P(), P()),
        check_vma=False,
    )
```

```python
import functools
import math

import jax
import jax.numpy as jnp
from jax import lax
from jax.experimental import pallas as pl
from jax.experimental.pallas import tpu as pltpu
from jax.sharding import PartitionSpec as P

H = 4
OWN_ROWS = 1024
BLOCK = 512
LEN = 256
TILE = 256

norm_eps = 1e-05
VMEM = pltpu.MemorySpace.VMEM
SMEM = pltpu.MemorySpace.SMEM
HBM = pltpu.MemorySpace.HBM


def dot_nn(a, b):
    return lax.dot_general(a, b, (((1,), (0,)), ((), ())), preferred_element_type=jnp.float32)


def dot_nt(a, b):
    return lax.dot_general(a, b, (((1,), (1,)), ((), ())), preferred_element_type=jnp.float32)


def dot_tn(a, b):
    return lax.dot_general(a, b, (((0,), (0,)), ((), ())), preferred_element_type=jnp.float32)


def sigmoid(z):
    return 0.5 * jnp.tanh(0.5 * z) + 0.5


def block_kernel(
    chunk, place, lengths, emb_hbm, cot_hbm, in_hbm, out_hbm,
    keep, send, grad_pre, rel_q, rel_r, rel_g,
    emb, cot, in_proj, out_proj, hid, dpre, mask, wts, dsc, att, gated_out, rel_p, sems,
):
    rows, width = emb.shape
    head = width // H
    scale = 1.0 / math.sqrt(head)
    copies = [pltpu.make_async_copy(emb_hbm, emb, sems.at[0])]
    for c in range(4):
        cols = pl.ds(c * width, width)
        copies.append(pltpu.make_async_copy(in_hbm.at[:, cols], in_proj.at[:, cols], sems.at[1 + c]))
    copies.append(pltpu.make_async_copy(cot_hbm, cot, sems.at[5]))
    copies.append(pltpu.make_async_copy(out_hbm, out_proj, sems.at[6]))
    for c in copies:
        c.start()
    along_lane = lax.broadcasted_iota(jnp.int32, (1, rows), 1)
    along_row = lax.broadcasted_iota(jnp.int32, (rows, 1), 0)
    end = jnp.int32(0)
    seg_lane, seg_row = jnp.zeros_like(along_lane), jnp.zeros_like(along_row)
    for s in range(lengths.shape[1]):
        end = end + lengths[0, s]
        seg_lane = seg_lane + (along_lane >= end).astype(jnp.int32)
        seg_row = seg_row + (along_row >= end).astype(jnp.int32)
    for i in range(rows // TILE):
        r, n = pl.ds(i * TILE, TILE), (i + 1) * TILE
        own = seg_row[i * TILE : n] == seg_lane[:, :n]
        past = along_lane[:, :n] <= along_row[i * TILE : n]
        mask[r, :n] = jnp.where(own & past, 1.0 / LEN, 0.0)
    copies[0].wait()
    for c in range(4):
        cols = pl.ds(c * width, width)
        copies[1 + c].wait()
        z = dot_nn(emb[...], in_proj[:, cols])
        sig = sigmoid(z)
        act = z * sig
        hid[:, cols] = act.astype(jnp.bfloat16)
        dpre[:, cols] = sig + act * (1.0 - sig)
    emb_t = emb[...].T
    count = width // chunk
    for c in range(count):
        for chain, rel in enumerate((rel_p, rel_q, rel_r)):
            rel[moved(c, place, chain, chunk), :] = emb_t[c * chunk : (c + 1) * chunk]
    for h in range(H):
        v, q, k = (pl.ds((c * H + h) * head, head) for c in (1, 2, 3))
        for i in range(rows // TILE):
            r, n = pl.ds(i * TILE, TILE), (i + 1) * TILE
            m = mask[r, :n]
            s = dot_nt(hid[r, q], hid[:n, k]) * scale
            sig = sigmoid(s)
            act = s * sig
            w = (act * m).astype(jnp.bfloat16)
            wts[h, r, :n] = w
            dsc[h, r, :n] = (sig + act * (1.0 - sig)) * m
            att[r, pl.ds(h * head, head)] = dot_nn(w, hid[:n, v])
    copies[5].wait()
    copies[6].wait()
    grad_att = []
    for i in range(rows // TILE):
        r = pl.ds(i * TILE, TILE)
        a = att[r, :]
        centered = a - jnp.mean(a, axis=1, keepdims=True)
        inv_std = lax.rsqrt(jnp.mean(centered * centered, axis=1, keepdims=True) + norm_eps)
        normed = centered * inv_std
        gating = hid[r, :width].astype(jnp.float32)
        gated_out[r, :] = (normed * gating).astype(jnp.bfloat16)
        grad_out = dot_nt(cot[r, :], out_proj[...])
        grad_pre[r, :width] = (grad_out * normed * dpre[r, :width]).astype(jnp.bfloat16)
        grad_norm = grad_out * gating
        g = inv_std * (
            grad_norm
            - jnp.mean(grad_norm, axis=1, keepdims=True)
            - normed * jnp.mean(grad_norm * normed, axis=1, keepdims=True)
        )
        grad_att.append(g.astype(jnp.bfloat16))
    gated_t = gated_out[...].T
    for c in range(count):
        rel_g[moved(c, place, 2, chunk), :] = gated_t[c * chunk : (c + 1) * chunk]
    for h in range(H):
        v, q, k = (pl.ds((c * H + h) * head, head) for c in (1, 2, 3))
        grad_v, grad_k = [None] * (rows // TILE), [None] * (rows // TILE)
        for i in range(rows // TILE):
            r, n = pl.ds(i * TILE, TILE), (i + 1) * TILE
            g = grad_att[i][:, h * head : (h + 1) * head]
            gs = (dot_nt(g, hid[:n, v]) * dsc[h, r, :n]).astype(jnp.bfloat16)
            gq = dot_nn(gs, hid[:n, k]) * scale
            grad_pre[r, q] = (gq * dpre[r, q]).astype(jnp.bfloat16)
            for j in range(i + 1):
                cut = slice(j * TILE, (j + 1) * TILE)
                gv = dot_tn(wts[h, r, cut], g)
                gk = dot_tn(gs[:, cut], hid[r, q])
                grad_v[j] = gv if grad_v[j] is None else grad_v[j] + gv
                grad_k[j] = gk if grad_k[j] is None else grad_k[j] + gk
        for j in range(rows // TILE):
            r = pl.ds(j * TILE, TILE)
            grad_pre[r, v] = (grad_v[j] * dpre[r, v]).astype(jnp.bfloat16)
            grad_pre[r, k] = (grad_k[j] * scale * dpre[r, k]).astype(jnp.bfloat16)
    half, cut = keep.shape
    keep[...] = dot_nn(rel_p[:half, :], grad_pre[:, :cut])
    send[...] = dot_nn(rel_p[half:, :], grad_pre[:, :cut])


def moved(c, place, chain, chunk):
    return pl.ds(pl.multiple_of((c ^ place[chain]) * chunk, chunk), chunk)


def block_call(chunk, cut, place, lengths, emb, cot, in_proj, out_proj):
    rows, width = emb.shape
    vmem = pl.BlockSpec(memory_space=VMEM)
    part = jax.ShapeDtypeStruct((width // 2, cut), jnp.float32)
    square = jax.ShapeDtypeStruct((width, rows), jnp.bfloat16)
    return pl.pallas_call(
        functools.partial(block_kernel, chunk),
        name="block",
        out_shape=(part, part, jax.ShapeDtypeStruct((rows, 4 * width), jnp.bfloat16), square, square, square),
        in_specs=[pl.BlockSpec(memory_space=SMEM)] * 2 + [pl.BlockSpec(memory_space=HBM)] * 4,
        out_specs=(vmem,) * 6,
        scratch_shapes=[
            pltpu.VMEM((rows, width), jnp.bfloat16),
            pltpu.VMEM((rows, width), jnp.bfloat16),
            pltpu.VMEM((width, 4 * width), jnp.bfloat16),
            pltpu.VMEM((width, width), jnp.bfloat16),
            pltpu.VMEM((rows, 4 * width), jnp.bfloat16),
            pltpu.VMEM((rows, 4 * width), jnp.float32),
            pltpu.VMEM((rows, rows), jnp.float32),
            pltpu.VMEM((H, rows, rows), jnp.bfloat16),
            pltpu.VMEM((H, rows, rows), jnp.float32),
            pltpu.VMEM((rows, width), jnp.float32),
            pltpu.VMEM((rows, width), jnp.bfloat16),
            pltpu.VMEM((width, rows), jnp.bfloat16),
            pltpu.SemaphoreType.DMA((7,)),
        ],
        compiler_params=pltpu.CompilerParams(vmem_limit_bytes=28 << 20),
    )(place, lengths, *(pltpu.with_memory_space_constraint(x, HBM) for x in (emb, cot, in_proj, out_proj)))


def rest_kernel(first, rel_q, rel_r, rel_g, cot, grad_pre, keep_q, send_q, keep_r, send_r):
    half, cut = keep_q.shape
    at = first + cut
    inner = grad_pre.shape[1] - at
    for keep, r in ((keep_q, pl.ds(0, half)), (send_q, pl.ds(half, half))):
        keep[...] = dot_nn(rel_q[r, :], grad_pre[:, first:at])
    for keep, r in ((keep_r, pl.ds(0, half)), (send_r, pl.ds(half, half))):
        if inner:
            keep[:, :inner] = dot_nn(rel_r[r, :], grad_pre[:, at:])
        keep[:, inner:] = dot_nn(rel_g[r, :], cot[...])


def rest_call(cuts, rel_q, rel_r, rel_g, cot, grad_pre):
    width = cot.shape[1]
    vmem = pl.BlockSpec(memory_space=VMEM)
    part_q, part_r = (jax.ShapeDtypeStruct((width // 2, n), jnp.float32) for n in cuts[1:])
    return pl.pallas_call(
        functools.partial(rest_kernel, cuts[0]),
        name="rest",
        out_shape=(part_q, part_q, part_r, part_r),
        in_specs=[vmem] * 5,
        out_specs=(vmem,) * 4,
        compiler_params=pltpu.CompilerParams(vmem_limit_bytes=8 << 20),
    )(rel_q, rel_r, rel_g, cot, grad_pre)


def split_bf16(x):
    high = x.astype(jnp.bfloat16)
    return high, (x - high.astype(jnp.float32)).astype(jnp.bfloat16)


def item_kernel(owners, slots, ids, cot, grad_pre, in_proj, sent):
    rows, width = cot.shape
    item_grad = dot_nt(grad_pre[...], in_proj[...]) + cot[...].astype(jnp.float32)
    high, low = split_bf16(item_grad)
    id_lane = ids[...]
    sub = lax.broadcasted_iota(jnp.int32, (rows, rows), 0)
    lane = lax.broadcasted_iota(jnp.int32, (rows, rows), 1)
    id_row = jnp.sum(jnp.where(sub == lane, id_lane, 0), axis=1, keepdims=True)
    repeat = jnp.max(jnp.where((id_row == id_lane) & (lane < sub), 1, 0), axis=1, keepdims=True)
    key = jnp.where(repeat == 0, id_row, jnp.int32(2**30))
    owner = id_lane // OWN_ROWS
    below = (key >= owner * OWN_ROWS) & (key < id_lane)
    rank = jnp.sum(jnp.where(below, 1, 0), axis=0, keepdims=True)
    slot = owner * slots + rank
    total = owners * slots
    pick = lax.broadcasted_iota(jnp.int32, (total, rows), 0) == slot
    onehot = jnp.where(pick, 1.0, 0.0).astype(jnp.bfloat16)
    summed = dot_nn(onehot, high) + dot_nn(onehot, low)
    for c in range(width // 128):
        sent[:, c * slots : (c + 1) * slots, :] = summed[:, c * 128 : (c + 1) * 128].reshape(owners, slots, 128)
    number = jnp.max(jnp.where(pick, id_lane - owner * OWN_ROWS, -1), axis=1, keepdims=True)
    number = jnp.broadcast_to(number.astype(jnp.float32), (total, 128)).reshape(owners, slots, 128)
    groups = slots // 8
    at = lax.broadcasted_iota(jnp.int32, (owners, 8, 128), 2) // (128 // groups)
    tail = number[:, :8]
    for g in range(1, groups):
        tail = jnp.where(at == g, number[:, g * 8 : (g + 1) * 8], tail)
    sent[:, (width // 128) * slots :, :] = tail


def item_call(owners, slots, ids, cot, grad_pre, in_proj):
    width = cot.shape[1]
    vmem = pl.BlockSpec(memory_space=VMEM)
    return pl.pallas_call(
        functools.partial(item_kernel, owners, slots),
        name="items",
        out_shape=jax.ShapeDtypeStruct((owners, (width // 128) * slots + 8, 128), jnp.float32),
        in_specs=[vmem] * 4,
        out_specs=vmem,
        compiler_params=pltpu.CompilerParams(vmem_limit_bytes=8 << 20),
    )(ids, cot, grad_pre, in_proj)


def table_kernel(owners, slots, got, emb_grad):
    width = emb_grad.shape[1]
    groups = slots // 8
    tail = got[:, (width // 128) * slots :, :]
    number = [tail[:, :, g * (128 // groups) : g * (128 // groups) + 1] for g in range(groups)]
    number = jnp.concatenate(number, axis=1).reshape(owners * slots, 1).astype(jnp.int32)
    pick = number == lax.broadcasted_iota(jnp.int32, (owners * slots, OWN_ROWS), 1)
    onehot = jnp.where(pick, 1.0, 0.0).astype(jnp.bfloat16).T
    for c in range(0, width // 128, 2):
        rows = [got[:, d * slots : (d + 1) * slots, :].reshape(owners * slots, 128) for d in (c, c + 1)]
        high, low = split_bf16(jnp.concatenate(rows, axis=1))
        emb_grad[:, c * 128 : (c + 2) * 128] = dot_nn(onehot, high) + dot_nn(onehot, low)


def table_call(owners, slots, got, width):
    vmem = pl.BlockSpec(memory_space=VMEM)
    return pl.pallas_call(
        functools.partial(table_kernel, owners, slots),
        name="table",
        out_shape=jax.ShapeDtypeStruct((OWN_ROWS, width), jnp.float32),
        in_specs=[vmem],
        out_specs=vmem,
        compiler_params=pltpu.CompilerParams(vmem_limit_bytes=8 << 20),
    )(got)


def place_kernel(chunk, spots, place, *refs):
    pieces, (in_grad, out_grad), sems = refs[: len(spots)], refs[-3:-1], refs[-1]
    copies = []
    for piece, (chain, first, position) in zip(pieces, spots):
        cut = piece.shape[1]
        inner = min(cut, in_grad.shape[1] - first)
        for c in range(piece.shape[0] // chunk):
            row = moved(position + c, place, chain, chunk)
            src = piece.at[pl.ds(c * chunk, chunk)]
            if inner:
                copies.append((src.at[:, pl.ds(0, inner)], in_grad.at[row, pl.ds(first, inner)]))
            if inner < cut:
                copies.append((src.at[:, pl.ds(inner, cut - inner)], out_grad.at[row, :]))
    copies = [pltpu.make_async_copy(s, d, sems.at[i]) for i, (s, d) in enumerate(copies)]
    for c in copies:
        c.start()
    for c in copies:
        c.wait()


def place_call(chunk, spots, place, pieces, width, grads):
    anywhere = pl.BlockSpec(memory_space=HBM)
    vmem = pl.BlockSpec(memory_space=VMEM)
    return pl.pallas_call(
        functools.partial(place_kernel, chunk, spots),
        name="place",
        out_shape=(
            jax.ShapeDtypeStruct((width, 4 * width), jnp.float32),
            jax.ShapeDtypeStruct((width, width), jnp.float32),
        ),
        in_specs=[pl.BlockSpec(memory_space=SMEM)] + [vmem] * len(pieces) + [anywhere] * len(grads),
        out_specs=(anywhere,) * 2,
        scratch_shapes=[pltpu.SemaphoreType.DMA((4 * width // chunk,))],
        input_output_aliases={1 + len(pieces) + i: i for i in range(len(grads))},
        compiler_params=pltpu.CompilerParams(vmem_limit_bytes=2 << 20),
    )(place, *pieces, *grads)


def swap(x, where):
    axis, distance = where
    size = lax.axis_size(axis)
    return lax.ppermute(x, axis, [(i, i ^ distance) for i in range(size)])


def bits_of(axis):
    return [(axis, 1 << b) for b in range(lax.axis_size(axis).bit_length() - 1)]


def orders():
    table = bits_of("table")
    core, rest, z = table[:1], table[1:], bits_of("dp")
    x, y = rest[: len(rest) // 2], rest[len(rest) // 2 :]
    z, last = z[:-1], z[-1:]
    return core + x + y + z + last, core + y + z + x + last, core + z + x + y + last


def position(order):
    at = jnp.int32(0)
    for axis, distance in order:
        at = 2 * at + (lax.axis_index(axis) // distance) % 2
    return at


def after(x, *others):
    return lax.optimization_barrier((x, *others))[0]


def apart(*xs):
    return lax.optimization_barrier(xs)


def halve(x):
    n = x.shape[0] // 2
    return apart(x[:n], x[n:])


def exchange(keep, send, order, scale):
    x = keep + (yield swap(send, order[0]))
    for where in order[1:-1]:
        keep, send = halve(x)
        x = keep + (yield swap(send, where))
    x = (x + (yield swap(x, order[-1]))) * scale
    for where in order[-2:1:-1]:
        (x,) = apart(x)
        x = jnp.concatenate([x, (yield swap(x, where))], axis=0)
    (x,) = apart(x)
    return x, swap(x, order[1]), swap(x, order[0])


class Run:
    def __init__(self, steps):
        self.steps, self.count, self.pieces, self.last = steps, 0, None, ()
        self.waiting = next(steps)

    def advance(self, *others):
        here = after(self.waiting, *others)
        self.count, self.last = self.count + 1, (here,)
        try:
            self.waiting = self.steps.send(here)
        except StopIteration as stop:
            self.pieces = stop.value


CUTS = 7, 8, 5
ITEMS_AT, SENT_AT, GOT_AT, TABLE_AT, STRICT = 1, 1, 3, 4, 1


def per_device(item_emb, cotangent, in_proj, out_proj, history_lengths, item_ids):
    rows_here, width = item_emb.shape
    owners = lax.axis_size("dp") * lax.axis_size("table")
    slots = max(8, rows_here // owners)
    order = orders()
    place = jnp.stack([position(o[:-1]) for o in order])
    chunk = width >> (len(order[0]) - 1)
    scale = 1.0 / math.sqrt(rows_here * owners)
    cuts = [c * 5 * width // 20 for c in CUTS]

    *p, grad_pre, rel_q, rel_r, rel_g = block_call(
        chunk, cuts[0], place, history_lengths, item_emb, cotangent, in_proj, out_proj
    )
    q_keep, q_send, *r = rest_call(cuts, rel_q, rel_r, rel_g, cotangent, grad_pre)
    runs = [Run(exchange(*x, o, scale)) for x, o in zip((p, (q_keep, q_send), r), order)]
    hold, got, emb_grad = (), None, None
    while runs[-1].pieces is None:
        step = runs[0].count
        if step == ITEMS_AT:
            sent = item_call(owners, slots, item_ids.reshape(1, rows_here), cotangent, grad_pre, in_proj)
            hold = (sent,)
        if step == SENT_AT:
            got = lax.all_to_all(after(sent, *(runs[0].last if SENT_AT > ITEMS_AT else ())), ("dp", "table"), split_axis=0, concat_axis=0, tiled=True)
        if step == TABLE_AT:
            emb_grad = table_call(owners, slots, after(got, *runs[0].last), width)
            hold = (emb_grad,)
        if step == GOT_AT:
            hold = (got,)
        for run in runs:
            run.advance(*hold)
            hold = run.last if step >= STRICT else hold
        hold = hold if step >= STRICT else ()
    if emb_grad is None:
        emb_grad = table_call(owners, slots, got, width)
    near, far, beside = zip(*(run.pieces for run in runs))
    firsts = [sum(cuts[:chain]) for chain in range(len(cuts))]
    quarter = width // chunk // 4
    spots = lambda at: [(chain, first, at * quarter) for chain, first in enumerate(firsts)]
    grads = place_call(chunk, spots(0) + spots(2), place, near + beside, width, ())
    far = [after(x, *grads, emb_grad) for x in far]
    across = [swap(x, o[0]) for x, o in zip(far, order)]
    in_grad, out_grad = place_call(chunk, spots(1) + spots(3), place, far + across, width, grads)
    return (emb_grad, in_grad, out_grad)


def solution(mesh):
    placed = (
        P(("dp", "table"), None),
        P(("dp", "table"), None),
        P(),
        P(),
        P(("dp", "table"), None),
        P(("dp", "table")),
    )
    return jax.shard_map(
        per_device,
        mesh=mesh,
        in_specs=placed,
        out_specs=(P(("dp", "table"), None), P(), P()),
        check_vma=False,
    )
```
